256 devices in a mesh: dp: 16 (over z, core), fsdp: 16 (over x, y).
Axes of the slice: x: 4, y: 4, z: 8, core: 2. Of those that a mesh axis runs over, the one named last changes fastest.
Arguments:
- normed: bfloat16 [98304, 4096], P(('dp', 'fsdp')), may hold values from -24 to 24
- queries: bfloat16 [98304, 2048], P(('dp', 'fsdp')), may hold values from -48 to 48
- key_rows: bfloat16 [98304, 512], P(('dp', 'fsdp')), may hold values from -6 to 6
- out_grad: bfloat16 [98304, 2048], P(('dp', 'fsdp')), may hold values from -6 to 6
- value_weight: bfloat16 [4096, 512], P('fsdp'), may hold values from -0.09375 to 0.09375
- doc_ids: int32 [256, 384], P(('dp', 'fsdp')), may hold values from 0 to 3, never falling along the last dimension, each value on 1 to 256 neighbouring positions
- send_to: int32 [256, 8], P(('dp', 'fsdp')), may hold values from 0 to 15, as said below
- take_from: int32 [256, 8], P(('dp', 'fsdp')), may hold values from 0 to 15, as said below
Outputs:
- query_grad: bfloat16 [98304, 2048], P(('dp', 'fsdp'))
- key_grad: bfloat16 [98304, 512], P(('dp', 'fsdp'))
- input_grad: bfloat16 [98304, 4096], P(('dp', 'fsdp'))
- weight_grad: float32 [4096, 512], P(('dp', 'fsdp'))
The draws below stay inside these ranges and needn't reach their ends.
Inputs may be any that keep to these rules, and one draw needn't show every extreme that they name: `send_to`: entry b of a device's row names the dp index of the device, with the same fsdp index, that packs this device's rows b * 48 to (b + 1) * 48 - 1; the 8 entries of a row are distinct, and every device packs exactly 8 blocks. `take_from`: entry p of a device's row names the dp index of the device whose block, sent to this device by send_to, becomes this device's packed rows p * 48 to (p + 1) * 48 - 1; the entries of a row are distinct, so one device sends at most one block to another. `doc_ids`: along a device's 384 rows document numbers never fall; a document holds at most 256 rows, and one document in every draw holds exactly that many.
All inputs are finite; a program needn't handle non-finite values.
Results may differ from the reference program's by a relative error of at most 0.006.
Values may be sent and summed in bfloat16 or wider, within the bound.
No kernel may reach another device: no remote copies, remote signals or barrier semaphores. Data moves between devices by JAX's collectives and lax.ppermute only.
A program may use at most 128 MiB of HBM per device.

```python
import math
import jax
import jax.numpy as jnp
import numpy as np
from jax import lax

D = 4096
HEADS = 16
KV_HEADS = 4
HEAD_DIM = 128
BLOCK_ROWS = 48
BLOCKS = 8
ROWS = 384
TOKENS = 98304
N_DP = 16
N_FSDP = 16


def random_perm(subkey, count_rows, width):
    scores = jax.random.randint(subkey, (count_rows, width), 0, 1 << 20) * width + jnp.arange(width, dtype=jnp.int32)[None, :]
    return jnp.argsort(scores, axis=1).astype(jnp.int32)


def plan_tables(key):
    source_perm = random_perm(jax.random.fold_in(key, 21), N_FSDP, N_DP)
    dest_perm = random_perm(jax.random.fold_in(key, 22), N_FSDP, N_DP)
    offsets = random_perm(jax.random.fold_in(key, 23), N_FSDP, N_DP)[:, :BLOCKS]
    source_inv = jnp.argsort(source_perm, axis=1).astype(jnp.int32)
    dest_inv = jnp.argsort(dest_perm, axis=1).astype(jnp.int32)
    position = (source_perm[:, :, None] + offsets[:, None, :]) % N_DP
    sending = jnp.take_along_axis(dest_perm, position.reshape(N_FSDP, N_DP * BLOCKS), axis=1).reshape(N_FSDP, N_DP, BLOCKS)
    send_table = jnp.transpose(sending, (1, 0, 2)).reshape(N_DP * N_FSDP, BLOCKS)
    back_pos = (dest_inv[:, :, None] - offsets[:, None, :]) % N_DP
    sources = jnp.take_along_axis(source_inv, back_pos.reshape(N_FSDP, N_DP * BLOCKS), axis=1).reshape(N_FSDP, N_DP, BLOCKS)
    slot_perm = random_perm(jax.random.fold_in(key, 24), N_FSDP * N_DP, BLOCKS).reshape(N_FSDP, N_DP, BLOCKS)
    taking = jnp.take_along_axis(sources, slot_perm, axis=2)
    take_table = jnp.transpose(taking, (1, 0, 2)).reshape(N_DP * N_FSDP, BLOCKS)
    return (send_table.astype(jnp.int32), take_table.astype(jnp.int32))


def base_keys(key):
    drawn = jnp.clip(jax.random.normal(jax.random.fold_in(key, 31), (TOKENS, KV_HEADS * HEAD_DIM), jnp.float32), -6.0, 6.0)
    return drawn


def draw_key_rows(key, part):
    return base_keys(key).astype(jnp.bfloat16)


def draw_queries(key, part):
    drawn = jnp.clip(jax.random.normal(jax.random.fold_in(key, 32), (TOKENS, HEADS * HEAD_DIM), jnp.float32), -6.0, 6.0)
    return drawn.astype(jnp.bfloat16)


def draw_send_to(key, part):
    return plan_tables(key)[0]


def draw_take_from(key, part):
    return plan_tables(key)[1]


def raised(result, key, source, target, parts, factor):
    def block_of(axis_at):
        return (jnp.arange(result.shape[axis_at]) // (result.shape[axis_at] // parts)).reshape((-1,) + (1,) * (result.ndim - 1 - axis_at))

    first = jax.random.permutation(key, parts)[block_of(target)]
    second = (block_of(target) + parts // 2) % parts
    return jnp.where((block_of(source) == first) | (block_of(source) == second), factor * result, result)


def levels(key, shape, split, smallest, largest):
    factor_of, own = 1.0, jax.random.fold_in(key, 6)
    for axis_at, blocks in split:
        heights = jnp.exp(jax.random.uniform(jax.random.fold_in(own, axis_at), (blocks,), jnp.float32, smallest / len(split), largest / len(split)))
        factor_of = factor_of * jnp.repeat(heights, shape[axis_at] // blocks).reshape([-1 if axis == axis_at else 1 for axis in range(len(shape))])
    return factor_of


def length_profile(number_of, total, limit, skew):
    loads = [(1 << 20) // math.isqrt(grade ** skew) + 1 for grade in range(2, number_of + 1)]
    spare, given = total - limit - (number_of - 1), [1] * (number_of - 1)
    while spare > 0:
        candidates = [i for i in range(number_of - 1) if given[i] < limit]
        pool, left = sum([loads[i] for i in candidates]), spare
        for i in candidates:
            extra = min(limit - given[i], max(1, left * loads[i] // pool), spare)
            given[i] = given[i] + extra
            spare = spare - extra
    return np.array([limit] + given)


def ragged_sizes(stream_key, amount, total, most, skew):
    if amount == 2:
        one = jax.random.randint(stream_key, (), max(1, total - most), min(most, total - 1) + 1)
        return jnp.stack([one, total - one])
    tallies = jnp.asarray(length_profile(amount, total, most, skew), jnp.int32)
    pairs = (amount - 1) // 2
    source_of, sink = tallies[1:1 + 2 * pairs:2], tallies[2:2 + 2 * pairs:2]
    margin = jnp.minimum(source_of - 1, most - sink)
    shifted = jax.random.randint(jax.random.fold_in(stream_key, 1), (pairs,), 0, 1 << 20) % (margin + 1)
    tallies = tallies.at[1:1 + 2 * pairs:2].set(source_of - shifted).at[2:2 + 2 * pairs:2].set(sink + shifted)
    return tallies[jax.random.permutation(jax.random.fold_in(stream_key, 2), amount)]


def centred(own_key, extent, spread, bound, shards=(), kind=jnp.bfloat16):
    gain = levels(own_key, extent, shards, -0.22, 0.18) if shards else 1.0
    values = jax.random.normal(own_key, extent, jnp.float32) * spread * gain
    return jnp.minimum(jnp.maximum(values, -bound), bound).astype(kind)


def noise_with(own_key, dims, scale, most, split, heavy, kind=jnp.bfloat16):
    values = scale * jax.random.normal(own_key, dims, jnp.float32)
    if split:
        values = values * levels(own_key, dims, split, -0.22, 0.18)
    return jnp.clip(raised(values, jax.random.fold_in(own_key, 3), *heavy), -most, most).astype(kind)


def setup_inputs(seed: int = 0) -> dict:
    key_of = jax.random.split(jax.random.key(seed), 9)
    return {
        "normed": noise_with(key_of[0], (TOKENS, D), 1.0, 24.0, ((0, 256),), (0, 1, 256, 6.0)),
        "queries": draw_queries(jax.random.fold_in(key_of[8], 71), 0),
        "key_rows": draw_key_rows(jax.random.fold_in(key_of[8], 71), 0),
        "out_grad": centred(key_of[3], (TOKENS, HEADS * HEAD_DIM), 1.0, 6.0, ((0, 256),)),
        "value_weight": centred(key_of[4], (D, KV_HEADS * HEAD_DIM), D ** -0.5, 0.09375, ((0, 16),)),
        "doc_ids": jax.vmap(lambda own: jnp.searchsorted(jnp.cumsum(ragged_sizes(own, 4, ROWS, 2 * ROWS // 3, 2)), jnp.arange(ROWS), side="right"))(jax.random.split(key_of[5], (N_DP * N_FSDP))).reshape((N_DP * N_FSDP, ROWS)).astype(jnp.int32),
        "send_to": draw_send_to(jax.random.fold_in(key_of[8], 71), 0),
        "take_from": draw_take_from(jax.random.fold_in(key_of[8], 71), 0),
    }


def reference(normed, queries, key_rows, out_grad, value_weight, doc_ids, send_to, take_from):
    group_size = HEADS // KV_HEADS
    score_scale = HEAD_DIM ** -0.5
    device_count = N_DP * N_FSDP
    values = jnp.dot(normed, value_weight, preferred_element_type=jnp.float32).astype(jnp.bfloat16)
    send_tab = send_to.reshape(N_DP, N_FSDP, BLOCKS)
    take_tab = take_from.reshape(N_DP, N_FSDP, BLOCKS)
    fsdp_index = jnp.arange(N_FSDP, dtype=jnp.int32)[None, :, None]
    dp_index = jnp.arange(N_DP, dtype=jnp.int32)[:, None, None]
    block_index = jnp.arange(BLOCKS, dtype=jnp.int32)
    source_rows = send_tab[take_tab, fsdp_index]
    source_block = jnp.sum(jnp.where(source_rows == dp_index[..., None], block_index, 0), axis=-1).astype(jnp.int32)
    dest_rows = take_tab[send_tab, fsdp_index]
    dest_block = jnp.sum(jnp.where(dest_rows == dp_index[..., None], block_index, 0), axis=-1).astype(jnp.int32)

    def to_packed(array):
        shaped = array.reshape(N_DP, N_FSDP, BLOCKS, BLOCK_ROWS, array.shape[1])
        return shaped[take_tab, fsdp_index, source_block].reshape(array.shape)

    def to_generator(array):
        shaped = array.reshape(N_DP, N_FSDP, BLOCKS, BLOCK_ROWS, array.shape[1])
        return shaped[send_tab, fsdp_index, dest_block].reshape(array.shape)

    packed_q = to_packed(queries)
    packed_k = to_packed(key_rows)
    packed_v = to_packed(values)

    def device_attention(inputs):
        dev_q, dev_k, dev_v, dev_grad, doc_row = inputs
        query_heads = dev_q.astype(jnp.float32).reshape(ROWS, KV_HEADS, group_size, HEAD_DIM)
        grad_heads = dev_grad.astype(jnp.float32).reshape(ROWS, KV_HEADS, group_size, HEAD_DIM)
        key_heads = dev_k.astype(jnp.float32).reshape(ROWS, KV_HEADS, HEAD_DIM)
        value_heads = dev_v.astype(jnp.float32).reshape(ROWS, KV_HEADS, HEAD_DIM)
        scores = jnp.einsum("igxd,jgd->gxij", query_heads, key_heads) * score_scale
        positions = jnp.arange(ROWS, dtype=jnp.int32)
        allowed = (doc_row[:, None] == doc_row[None, :]) & (positions[None, :] <= positions[:, None])
        masked = jnp.where(allowed, scores, -jnp.inf)
        row_peak = jnp.max(masked, axis=-1, keepdims=True)
        exponent = jnp.exp(masked - row_peak)
        attn_probs = exponent / jnp.sum(exponent, axis=-1, keepdims=True)
        probs_half = attn_probs.astype(jnp.bfloat16).astype(jnp.float32)
        attn_out = jnp.einsum("gxij,jgd->igxd", probs_half, value_heads)
        delta_rows = jnp.sum(grad_heads * attn_out, axis=-1)
        prob_grad = jnp.einsum("igxd,jgd->gxij", grad_heads, value_heads)
        score_grad = (attn_probs * (prob_grad - jnp.transpose(delta_rows, (1, 2, 0))[..., None]) * score_scale)
        score_grad = score_grad.astype(jnp.bfloat16).astype(jnp.float32)
        query_grad = jnp.einsum("gxij,jgd->igxd", score_grad, key_heads).astype(jnp.bfloat16).reshape(ROWS, -1)
        key_grad = jnp.einsum("gxij,igxd->jgd", score_grad, query_heads).astype(jnp.bfloat16).reshape(ROWS, -1)
        value_grad = jnp.einsum("gxij,igxd->jgd", probs_half, grad_heads).astype(jnp.bfloat16).reshape(ROWS, -1)
        return query_grad, key_grad, value_grad

    results = lax.map(device_attention, (packed_q.reshape(device_count, ROWS, -1), packed_k.reshape(device_count, ROWS, -1), packed_v.reshape(device_count, ROWS, -1), out_grad.reshape(device_count, ROWS, -1), doc_ids))
    query_grad = results[0].reshape(TOKENS, -1)
    key_grad = results[1].reshape(TOKENS, -1)
    value_grad = results[2].reshape(TOKENS, -1)
    input_grad = jnp.dot(value_grad, value_weight.T, preferred_element_type=jnp.float32).astype(jnp.bfloat16)
    value_home = to_generator(value_grad)
    weight_grad = jnp.dot(normed.T, value_home, preferred_element_type=jnp.float32) * (TOKENS ** -0.5)
    return query_grad, key_grad, input_grad, weight_grad
```

```python
import jax
import jax.numpy as jnp
from jax import lax
from jax.experimental import pallas as pl
from jax.experimental.pallas import tpu as pltpu
from jax.sharding import PartitionSpec as P

HEADS = 16
KV_HEADS = 4
HEAD_DIM = 128
GROUP = HEADS // KV_HEADS
BLOCK_ROWS = 48
QUERY_TILE = 128


def outgoing_kernel(send, q_ref, k_ref, out_ref):
    width = q_ref.shape[1]
    out_ref[0, :, :width] = q_ref[...]
    out_ref[0, :, width:] = k_ref[...]


def outgoing_slots(send, queries, key_rows, peers):
    rows, width = queries.shape
    key_width = key_rows.shape[1]
    blocks = rows // BLOCK_ROWS
    return pl.pallas_call(
        outgoing_kernel,
        grid_spec=pltpu.PrefetchScalarGridSpec(
            num_scalar_prefetch=1,
            grid=(blocks,),
            in_specs=[
                pl.BlockSpec((BLOCK_ROWS, width), lambda b, send: (b, 0)),
                pl.BlockSpec((BLOCK_ROWS, key_width), lambda b, send: (b, 0)),
            ],
            out_specs=pl.BlockSpec(
                (1, BLOCK_ROWS, width + key_width), lambda b, send: (send[b], 0, 0)
            ),
        ),
        out_shape=jax.ShapeDtypeStruct((peers, BLOCK_ROWS, width + key_width), queries.dtype),
        name="outgoing_slots",
    )(send, queries, key_rows)


def values_kernel(send, normed_ref, weight_ref, out_ref, total):
    step = pl.program_id(0)
    part = jnp.dot(normed_ref[...], weight_ref[...], preferred_element_type=jnp.float32)

    @pl.when(step == 0)
    def _():
        total[...] = part

    @pl.when(step > 0)
    def _():
        total[...] += part

    @pl.when(step == pl.num_programs(0) - 1)
    def _():
        for b in range(total.shape[0] // BLOCK_ROWS):
            rows = total[b * BLOCK_ROWS : (b + 1) * BLOCK_ROWS, :]
            out_ref[send[b]] = rows.astype(out_ref.dtype)


def value_slots(send, normed, weight, peers):
    rows, depth = normed.shape
    width = weight.shape[1]
    tile = 512
    return pl.pallas_call(
        values_kernel,
        grid_spec=pltpu.PrefetchScalarGridSpec(
            num_scalar_prefetch=1,
            grid=(depth // tile,),
            in_specs=[
                pl.BlockSpec((rows, tile), lambda k, send: (0, k)),
                pl.BlockSpec((tile, width), lambda k, send: (k, 0)),
            ],
            out_specs=pl.BlockSpec((peers, BLOCK_ROWS, width), lambda k, send: (0, 0, 0)),
            scratch_shapes=[pltpu.VMEM((rows, width), jnp.float32)],
        ),
        out_shape=jax.ShapeDtypeStruct((peers, BLOCK_ROWS, width), normed.dtype),
        name="value_slots",
    )(send, normed, weight)


def attention_kernel(
    take, q_ref, k_ref, v_ref, grad_ref, doc_row, doc_col,
    query_grad, key_grad, value_grad, returning,
    q_rows, k_rows, v_rows, bias, key_total, value_total,
):
    rows = grad_ref.shape[0]
    blocks = rows // BLOCK_ROWS
    scale = HEAD_DIM ** (-0.5)

    @pl.when(pl.program_id(0) == 0)
    def _():
        i = lax.broadcasted_iota(jnp.int32, (rows, rows), 0)
        j = lax.broadcasted_iota(jnp.int32, (rows, rows), 1)
        allowed = (doc_col[...] == doc_row[...]) & (j <= i)
        bias[...] = jnp.where(allowed, 0.0, -jnp.inf)

    for p in range(blocks):
        place = slice(p * BLOCK_ROWS, (p + 1) * BLOCK_ROWS)
        q_rows[place, :] = q_ref[take[p]]
        k_rows[place, :] = k_ref[take[p]]
        v_rows[place, :] = v_ref[take[p]]

    key_total[...] = jnp.zeros_like(key_total)
    value_total[...] = jnp.zeros_like(value_total)
    for start in range(0, rows, QUERY_TILE):
        place = slice(start, start + QUERY_TILE)
        reach = start + QUERY_TILE
        q = jnp.concatenate(
            [q_rows[place, x * HEAD_DIM : (x + 1) * HEAD_DIM] for x in range(GROUP)], axis=0
        )
        g = jnp.concatenate(
            [grad_ref[place, x * HEAD_DIM : (x + 1) * HEAD_DIM] for x in range(GROUP)], axis=0
        )
        k = k_rows[:reach, :]
        v = v_rows[:reach, :]
        nt = (((1,), (1,)), ((), ()))
        tn = (((0,), (0,)), ((), ()))
        scores = lax.dot_general(q, k, nt, preferred_element_type=jnp.float32) * scale
        hide = bias[place, :reach]
        scores = scores + jnp.concatenate([hide] * GROUP, axis=0)
        peak = jnp.max(scores, axis=-1, keepdims=True)
        exponent = jnp.exp(scores - peak)
        probs = exponent / jnp.sum(exponent, axis=-1, keepdims=True)
        half = probs.astype(jnp.bfloat16)
        attn = jnp.dot(half, v, preferred_element_type=jnp.float32)
        delta = jnp.sum(g.astype(jnp.float32) * attn, axis=-1, keepdims=True)
        prob_grad = lax.dot_general(g, v, nt, preferred_element_type=jnp.float32)
        score_grad = (probs * (prob_grad - delta) * scale).astype(jnp.bfloat16)
        back = jnp.dot(score_grad, k, preferred_element_type=jnp.float32)
        for x in range(GROUP):
            query_grad[place, x * HEAD_DIM : (x + 1) * HEAD_DIM] = back[
                x * QUERY_TILE : (x + 1) * QUERY_TILE
            ].astype(query_grad.dtype)
        key_total[:reach, :] += lax.dot_general(
            score_grad, q, tn, preferred_element_type=jnp.float32
        )
        value_total[:reach, :] += lax.dot_general(half, g, tn, preferred_element_type=jnp.float32)
    key_grad[...] = key_total[...].astype(key_grad.dtype)
    value_grad[...] = value_total[...].astype(value_grad.dtype)
    returning[...] = jnp.zeros_like(returning)
    for p in range(blocks):
        place = slice(p * BLOCK_ROWS, (p + 1) * BLOCK_ROWS)
        returning[take[p]] = value_total[place, :].astype(returning.dtype)


def attention(take, arrived, arrived_v, out_grad, doc_ids):
    peers = arrived.shape[0]
    rows = out_grad.shape[0]
    wide = GROUP * HEAD_DIM
    first_key = HEADS
    bf16 = jnp.bfloat16
    return pl.pallas_call(
        attention_kernel,
        grid_spec=pltpu.PrefetchScalarGridSpec(
            num_scalar_prefetch=1,
            grid=(KV_HEADS,),
            in_specs=[
                pl.BlockSpec((peers, BLOCK_ROWS, wide), lambda g, take: (0, 0, g)),
                pl.BlockSpec((peers, BLOCK_ROWS, HEAD_DIM), lambda g, take: (0, 0, first_key + g)),
                pl.BlockSpec((peers, BLOCK_ROWS, HEAD_DIM), lambda g, take: (0, 0, g)),
                pl.BlockSpec((rows, wide), lambda g, take: (0, g)),
                pl.BlockSpec((1, rows), lambda g, take: (0, 0)),
                pl.BlockSpec((rows, 1), lambda g, take: (0, 0)),
            ],
            out_specs=[
                pl.BlockSpec((rows, wide), lambda g, take: (0, g)),
                pl.BlockSpec((rows, HEAD_DIM), lambda g, take: (0, g)),
                pl.BlockSpec((rows, HEAD_DIM), lambda g, take: (0, g)),
                pl.BlockSpec((peers, BLOCK_ROWS, HEAD_DIM), lambda g, take: (0, 0, g)),
            ],
            scratch_shapes=[
                pltpu.VMEM((rows, wide), bf16),
                pltpu.VMEM((rows, HEAD_DIM), bf16),
                pltpu.VMEM((rows, HEAD_DIM), bf16),
                pltpu.VMEM((rows, rows), jnp.float32),
                pltpu.VMEM((rows, HEAD_DIM), jnp.float32),
                pltpu.VMEM((rows, HEAD_DIM), jnp.float32),
            ],
        ),
        out_shape=[
            jax.ShapeDtypeStruct((rows, KV_HEADS * wide), bf16),
            jax.ShapeDtypeStruct((rows, KV_HEADS * HEAD_DIM), bf16),
            jax.ShapeDtypeStruct((rows, KV_HEADS * HEAD_DIM), bf16),
            jax.ShapeDtypeStruct((peers, BLOCK_ROWS, KV_HEADS * HEAD_DIM), bf16),
        ],
        name="attention_backward",
    )(take, arrived, arrived, arrived_v, out_grad, doc_ids, doc_ids.reshape(rows, 1))


def weight_kernel(send, place, normed_ref, landed_ref, out_ref, home):
    @pl.when(pl.program_id(0) == 0)
    def _():
        for b in range(home.shape[0] // BLOCK_ROWS):
            home[b * BLOCK_ROWS : (b + 1) * BLOCK_ROWS, :] = landed_ref[send[b]]

    part = lax.dot_general(
        normed_ref[...], home[...], (((0,), (0,)), ((), ())), preferred_element_type=jnp.float32
    )
    out_ref[...] = part.reshape(out_ref.shape).astype(out_ref.dtype)


def weight_part(send, place, normed, landed, columns):
    rows, depth = normed.shape
    peers, _, width = landed.shape
    steps = place.shape[0]
    tile = depth // peers
    share = tile // columns
    return pl.pallas_call(
        weight_kernel,
        grid_spec=pltpu.PrefetchScalarGridSpec(
            num_scalar_prefetch=2,
            grid=(steps,),
            in_specs=[
                pl.BlockSpec((rows, tile), lambda z, send, place: (0, place[z])),
                pl.BlockSpec((peers, BLOCK_ROWS, width), lambda z, send, place: (0, 0, 0)),
            ],
            out_specs=pl.BlockSpec(
                (columns, 1, share, width), lambda z, send, place: (0, z, 0, 0)
            ),
            scratch_shapes=[pltpu.VMEM((rows, width), jnp.bfloat16)],
        ),
        out_shape=jax.ShapeDtypeStruct((columns, steps, share, width), jnp.bfloat16),
        name="weight_part",
    )(send, place, normed, landed)


def local(normed, queries, key_rows, out_grad, value_weight, doc_ids, send_to, take_from):
    dp_count = lax.axis_size("dp")
    fsdp_count = lax.axis_size("fsdp")
    rows = normed.shape[0]
    grad_scale = (rows * dp_count * fsdp_count) ** (-0.5)
    send, take = send_to[0], take_from[0]
    core = lax.axis_index("dp") % 2

    arrived = lax.all_to_all(
        outgoing_slots(send, queries, key_rows, dp_count), "dp", 0, 0, tiled=True
    )
    weight = lax.all_gather(value_weight, "fsdp", axis=0, tiled=True)
    arrived_v = lax.all_to_all(
        value_slots(send, normed, weight, dp_count), "dp", 0, 0, tiled=True
    )
    query_grad, key_grad, value_grad, returning = attention(
        take, arrived, arrived_v, out_grad, doc_ids
    )
    landed = lax.all_to_all(returning, "dp", 0, 0, tiled=True)
    input_grad = lax.dot_general(
        value_grad, weight, (((1,), (1,)), ((), ())), preferred_element_type=jnp.float32
    ).astype(jnp.bfloat16)

    steps = dp_count // 2
    pairs = 2 * jnp.arange(steps, dtype=jnp.int32)
    theirs = weight_part(send, pairs + (1 - core), normed, landed, fsdp_count)
    swapped = lax.ppermute(theirs, "dp", [(i, i ^ 1) for i in range(dp_count)])
    mine = weight_part(send, pairs + core, normed, landed, fsdp_count)
    chip = (mine.astype(jnp.float32) + swapped.astype(jnp.float32)).astype(jnp.bfloat16)
    chips = lax.all_to_all(chip, "fsdp", 0, 0, tiled=True)
    plane = jnp.sum(chips.astype(jnp.float32), axis=0).astype(jnp.bfloat16)
    groups = [list(range(c, dp_count, 2)) for c in range(2)]
    planes = lax.all_to_all(plane, "dp", 0, 0, axis_index_groups=groups, tiled=True)
    weight_grad = jnp.sum(planes.astype(jnp.float32), axis=0) * grad_scale
    return (query_grad, key_grad, input_grad, weight_grad)


def solution(mesh):
    rows = P(("dp", "fsdp"), None)
    return jax.shard_map(
        local,
        mesh=mesh,
        in_specs=(rows, rows, rows, rows, P("fsdp", None), rows, rows, rows),
        out_specs=(rows, rows, rows, rows),
        check_vma=False,
    )
```

```python
import jax
import jax.numpy as jnp
from jax import lax
from jax.experimental import pallas as pl
from jax.experimental.pallas import tpu as pltpu
from jax.sharding import PartitionSpec as P


HEADS = 16
KV_HEADS = 4
HEAD_DIM = 128
GROUP = HEADS // KV_HEADS
BLOCK_ROWS = 48
QUERY_TILE = 128


def outgoing_kernel(send, q_ref, k_ref, out_ref):
    width = q_ref.shape[1]
    out_ref[0, :, :width] = q_ref[...]
    out_ref[0, :, width:] = k_ref[...]


def outgoing_slots(send, queries, key_rows, peers):
    rows, width = queries.shape
    key_width = key_rows.shape[1]
    blocks = rows // BLOCK_ROWS
    return pl.pallas_call(
        outgoing_kernel,
        grid_spec=pltpu.PrefetchScalarGridSpec(
            num_scalar_prefetch=1,
            grid=(blocks,),
            in_specs=[
                pl.BlockSpec((BLOCK_ROWS, width), lambda b, send: (b, 0)),
                pl.BlockSpec((BLOCK_ROWS, key_width), lambda b, send: (b, 0)),
            ],
            out_specs=pl.BlockSpec(
                (1, BLOCK_ROWS, width + key_width), lambda b, send: (send[b], 0, 0)
            ),
        ),
        out_shape=jax.ShapeDtypeStruct((peers, BLOCK_ROWS, width + key_width), queries.dtype),
        name="outgoing_slots",
    )(send, queries, key_rows)


def halves(core, ref, width):
    own = ref.at[:, pl.ds(pl.multiple_of(core * width, width), width)]
    other = ref.at[:, pl.ds(pl.multiple_of((1 - core) * width, width), width)]
    return own, other


def values_kernel(core, piece, block, normed_ref, own_ref, other_ref, *rest):
    outs, total = rest[:-1], rest[-1]
    step = pl.program_id(0)
    width = own_ref.shape[2]
    own, other = halves(core[0], total, width)

    @pl.when(step == 0)
    def _():
        total[...] = jnp.zeros_like(total)

    rows = normed_ref[...]
    own[...] += jnp.dot(rows, own_ref[0], preferred_element_type=jnp.float32)
    other[...] += jnp.dot(rows, other_ref[0], preferred_element_type=jnp.float32)

    @pl.when(step == pl.num_programs(0) - 1)
    def _():
        for o, out in enumerate(outs):
            first = pl.multiple_of(block[o] * BLOCK_ROWS, 16)
            out[...] = total[pl.ds(first, BLOCK_ROWS), :].astype(out.dtype)


def value_blocks(core, piece, block, normed, own, other):
    rows, _ = normed.shape
    pieces, tile, width = own.shape
    slots = block.shape[0]
    return pl.pallas_call(
        values_kernel,
        grid_spec=pltpu.PrefetchScalarGridSpec(
            num_scalar_prefetch=3,
            grid=(pieces,),
            in_specs=[
                pl.BlockSpec((rows, tile), lambda k, core, piece, block: (0, piece[k])),
                pl.BlockSpec((1, tile, width), lambda k, *_: (k, 0, 0)),
                pl.BlockSpec((1, tile, width), lambda k, *_: (k, 0, 0)),
            ],
            out_specs=[pl.BlockSpec((BLOCK_ROWS, 2 * width), lambda k, *_: (0, 0))] * slots,
            scratch_shapes=[pltpu.VMEM((rows, 2 * width), jnp.float32)],
        ),
        out_shape=[jax.ShapeDtypeStruct((BLOCK_ROWS, 2 * width), normed.dtype)] * slots,
        cost_estimate=pl.CostEstimate(
            flops=4 * rows * width * tile * pieces,
            bytes_accessed=2 * (normed.size + own.size + other.size),
            transcendentals=0,
        ),
        name="value_blocks",
    )(core, piece, block, normed, own, other)


def pack_kernel(place, *refs):
    out = refs[-1]
    for o, ref in enumerate(refs[:-1]):

        @pl.when(place[o] >= 0)
        def _():
            first = pl.multiple_of(place[o] * BLOCK_ROWS, 16)
            out[pl.ds(first, BLOCK_ROWS), :] = ref[...]


def pack(place, blocks, rows):
    width = blocks[0].shape[1]
    return pl.pallas_call(
        pack_kernel,
        grid_spec=pltpu.PrefetchScalarGridSpec(
            num_scalar_prefetch=1,
            grid=(1,),
            in_specs=[pl.BlockSpec((BLOCK_ROWS, width), lambda k, place: (0, 0))] * len(blocks),
            out_specs=pl.BlockSpec((rows, width), lambda k, place: (0, 0)),
        ),
        out_shape=jax.ShapeDtypeStruct((rows, width), blocks[0].dtype),
        name="pack_values",
    )(place, *blocks)


def pick_kernel(column, in_ref, out_ref):
    out_ref[...] = in_ref[...]


def pick_columns(column, array, tile):
    rows = array.shape[0]
    steps = column.shape[0]
    return pl.pallas_call(
        pick_kernel,
        grid_spec=pltpu.PrefetchScalarGridSpec(
            num_scalar_prefetch=1,
            grid=(steps,),
            in_specs=[pl.BlockSpec((rows, tile), lambda z, column: (0, column[z]))],
            out_specs=pl.BlockSpec((rows, tile), lambda z, column: (0, z)),
        ),
        out_shape=jax.ShapeDtypeStruct((rows, tile * steps), array.dtype),
        name="pick_columns",
    )(column, array)


def turn_kernel(column, own_ref, got_ref, out_ref):
    rows = own_ref.shape[0]
    out_ref[:, :rows] = own_ref[...].T
    out_ref[:, rows:] = got_ref[...].T


def turn_columns(column, array, got, tile):
    rows = array.shape[0]
    steps = column.shape[0]
    return pl.pallas_call(
        turn_kernel,
        grid_spec=pltpu.PrefetchScalarGridSpec(
            num_scalar_prefetch=1,
            grid=(steps,),
            in_specs=[
                pl.BlockSpec((rows, tile), lambda z, column: (0, column[z])),
                pl.BlockSpec((rows, tile), lambda z, column: (0, z)),
            ],
            out_specs=pl.BlockSpec((tile, 2 * rows), lambda z, column: (z, 0)),
        ),
        out_shape=jax.ShapeDtypeStruct((tile * steps, 2 * rows), array.dtype),
        name="turn_columns",
    )(column, array, got)


def input_grad_kernel(core, piece, grad_ref, own_ref, other_ref, out_ref):
    own, other = halves(core[0], grad_ref, own_ref.shape[2])
    nt = (((1,), (1,)), ((), ()))
    total = lax.dot_general(own[...], own_ref[0], nt, preferred_element_type=jnp.float32)
    total += lax.dot_general(other[...], other_ref[0], nt, preferred_element_type=jnp.float32)
    out_ref[...] = total.astype(out_ref.dtype)


def input_gradient(core, piece, value_grad, own, other):
    rows = value_grad.shape[0]
    pieces, tile, width = own.shape
    return pl.pallas_call(
        input_grad_kernel,
        grid_spec=pltpu.PrefetchScalarGridSpec(
            num_scalar_prefetch=2,
            grid=(pieces,),
            in_specs=[
                pl.BlockSpec((rows, 2 * width), lambda k, *_: (0, 0)),
                pl.BlockSpec((1, tile, width), lambda k, *_: (k, 0, 0)),
                pl.BlockSpec((1, tile, width), lambda k, *_: (k, 0, 0)),
            ],
            out_specs=pl.BlockSpec((rows, tile), lambda k, core, piece: (0, piece[k])),
        ),
        out_shape=jax.ShapeDtypeStruct((rows, tile * pieces), value_grad.dtype),
        cost_estimate=pl.CostEstimate(
            flops=4 * rows * width * tile * pieces,
            bytes_accessed=2 * (rows * tile * pieces + own.size + other.size),
            transcendentals=0,
        ),
        name="input_gradient",
    )(core, piece, value_grad, own, other)


def attention_kernel(
    take, q_ref, k_ref, v_ref, grad_ref, doc_row, doc_col,
    query_grad, key_grad, value_grad, returning,
    q_rows, k_rows, bias, key_total, value_total,
):
    rows = grad_ref.shape[0]
    blocks = rows // BLOCK_ROWS
    scale = HEAD_DIM ** (-0.5)

    @pl.when(pl.program_id(0) == 0)
    def _():
        i = lax.broadcasted_iota(jnp.int32, (rows, rows), 0)
        j = lax.broadcasted_iota(jnp.int32, (rows, rows), 1)
        allowed = (doc_col[...] == doc_row[...]) & (j <= i)
        bias[...] = jnp.where(allowed, 0.0, -jnp.inf)

    for p in range(blocks):
        place = slice(p * BLOCK_ROWS, (p + 1) * BLOCK_ROWS)
        q_rows[place, :] = q_ref[take[p]]
        k_rows[place, :] = k_ref[take[p]]

    key_total[...] = jnp.zeros_like(key_total)
    value_total[...] = jnp.zeros_like(value_total)
    for start in range(0, rows, QUERY_TILE):
        place = slice(start, start + QUERY_TILE)
        reach = start + QUERY_TILE
        q = jnp.concatenate(
            [q_rows[place, x * HEAD_DIM : (x + 1) * HEAD_DIM] for x in range(GROUP)], axis=0
        )
        g = jnp.concatenate(
            [grad_ref[place, x * HEAD_DIM : (x + 1) * HEAD_DIM] for x in range(GROUP)], axis=0
        )
        k = k_rows[:reach, :]
        v = v_ref[:reach, :]
        nt = (((1,), (1,)), ((), ()))
        tn = (((0,), (0,)), ((), ()))
        scores = lax.dot_general(q, k, nt, preferred_element_type=jnp.float32) * scale
        hide = bias[place, :reach]
        scores = scores + jnp.concatenate([hide] * GROUP, axis=0)
        peak = jnp.max(scores, axis=-1, keepdims=True)
        exponent = jnp.exp(scores - peak)
        probs = exponent / jnp.sum(exponent, axis=-1, keepdims=True)
        half = probs.astype(jnp.bfloat16)
        attn = jnp.dot(half, v, preferred_element_type=jnp.float32)
        delta = jnp.sum(g.astype(jnp.float32) * attn, axis=-1, keepdims=True)
        prob_grad = lax.dot_general(g, v, nt, preferred_element_type=jnp.float32)
        score_grad = (probs * (prob_grad - delta) * scale).astype(jnp.bfloat16)
        back = jnp.dot(score_grad, k, preferred_element_type=jnp.float32)
        for x in range(GROUP):
            query_grad[place, x * HEAD_DIM : (x + 1) * HEAD_DIM] = back[
                x * QUERY_TILE : (x + 1) * QUERY_TILE
            ].astype(query_grad.dtype)
        key_total[:reach, :] += lax.dot_general(
            score_grad, q, tn, preferred_element_type=jnp.float32
        )
        value_total[:reach, :] += lax.dot_general(half, g, tn, preferred_element_type=jnp.float32)
    key_grad[...] = key_total[...].astype(key_grad.dtype)
    value_grad[...] = value_total[...].astype(value_grad.dtype)
    returning[...] = jnp.zeros_like(returning)
    for p in range(blocks):
        place = slice(p * BLOCK_ROWS, (p + 1) * BLOCK_ROWS)
        returning[take[p]] = value_total[place, :].astype(returning.dtype)


def attention(take, arrived, packed_v, out_grad, doc_ids):
    peers = arrived.shape[0]
    rows = out_grad.shape[0]
    wide = GROUP * HEAD_DIM
    first_key = HEADS
    bf16 = jnp.bfloat16
    return pl.pallas_call(
        attention_kernel,
        grid_spec=pltpu.PrefetchScalarGridSpec(
            num_scalar_prefetch=1,
            grid=(KV_HEADS,),
            in_specs=[
                pl.BlockSpec((peers, BLOCK_ROWS, wide), lambda g, take: (0, 0, g)),
                pl.BlockSpec((peers, BLOCK_ROWS, HEAD_DIM), lambda g, take: (0, 0, first_key + g)),
                pl.BlockSpec((rows, HEAD_DIM), lambda g, take: (0, g)),
                pl.BlockSpec((rows, wide), lambda g, take: (0, g)),
                pl.BlockSpec((1, rows), lambda g, take: (0, 0)),
                pl.BlockSpec((rows, 1), lambda g, take: (0, 0)),
            ],
            out_specs=[
                pl.BlockSpec((rows, wide), lambda g, take: (0, g)),
                pl.BlockSpec((rows, HEAD_DIM), lambda g, take: (0, g)),
                pl.BlockSpec((rows, HEAD_DIM), lambda g, take: (0, g)),
                pl.BlockSpec((peers, BLOCK_ROWS, HEAD_DIM), lambda g, take: (0, 0, g)),
            ],
            scratch_shapes=[
                pltpu.VMEM((rows, wide), bf16),
                pltpu.VMEM((rows, HEAD_DIM), bf16),
                pltpu.VMEM((rows, rows), jnp.float32),
                pltpu.VMEM((rows, HEAD_DIM), jnp.float32),
                pltpu.VMEM((rows, HEAD_DIM), jnp.float32),
            ],
        ),
        out_shape=[
            jax.ShapeDtypeStruct((rows, KV_HEADS * wide), bf16),
            jax.ShapeDtypeStruct((rows, KV_HEADS * HEAD_DIM), bf16),
            jax.ShapeDtypeStruct((rows, KV_HEADS * HEAD_DIM), bf16),
            jax.ShapeDtypeStruct((peers, BLOCK_ROWS, KV_HEADS * HEAD_DIM), bf16),
        ],
        name="attention_backward",
    )(take, arrived, arrived, packed_v, out_grad, doc_ids, doc_ids.reshape(rows, 1))


def weight_kernel(send, turned_ref, landed_ref, swapped_ref, out_ref, home):
    rows = home.shape[0] // 2

    @pl.when(pl.program_id(0) == 0)
    def _():
        for b in range(rows // BLOCK_ROWS):
            place = slice(b * BLOCK_ROWS, (b + 1) * BLOCK_ROWS)
            home[place, :] = landed_ref[send[0, b]]
        for b in range(rows // BLOCK_ROWS):
            place = slice(rows + b * BLOCK_ROWS, rows + (b + 1) * BLOCK_ROWS)
            home[place, :] = swapped_ref[send[1, b]]

    part = jnp.dot(turned_ref[...], home[...], preferred_element_type=jnp.float32)
    out_ref[...] = part.reshape(out_ref.shape).astype(out_ref.dtype)


def weight_part(send, turned, landed, swapped, columns, steps):
    depth, rows = turned.shape
    peers, _, width = landed.shape
    tile = depth // steps
    share = tile // columns
    return pl.pallas_call(
        weight_kernel,
        grid_spec=pltpu.PrefetchScalarGridSpec(
            num_scalar_prefetch=1,
            grid=(steps,),
            in_specs=[
                pl.BlockSpec((tile, rows), lambda z, send: (z, 0)),
                pl.BlockSpec((peers, BLOCK_ROWS, width), lambda z, send: (0, 0, 0)),
                pl.BlockSpec((peers, BLOCK_ROWS, width), lambda z, send: (0, 0, 0)),
            ],
            out_specs=pl.BlockSpec((columns, 1, share, width), lambda z, send: (0, z, 0, 0)),
            scratch_shapes=[pltpu.VMEM((rows, width), jnp.bfloat16)],
        ),
        out_shape=jax.ShapeDtypeStruct((columns, steps, share, width), jnp.bfloat16),
        name="weight_part",
    )(send, turned, landed, swapped)


def grid_offsets(outer, inner):
    far = [(i, j) for i in range(outer) for j in range(inner)]
    reach = lambda o: -(min(o[0], outer - o[0]) + min(o[1], inner - o[1]))
    return sorted(far, key=lambda o: (reach(o), o))


def shift(index, offset, outer, inner, sign):
    i = (index // inner + sign * offset[0]) % outer
    j = (index % inner + sign * offset[1]) % inner
    return i * inner + j


def exchange(arrays, axis, offsets, outer, inner):
    moved = []
    for array, offset in zip(arrays, offsets):
        if offset == (0, 0):
            moved.append(array)
            continue
        pairs = [(i, shift(i, offset, outer, inner, 1)) for i in range(outer * inner)]
        moved.append(lax.ppermute(array, axis, pairs))
    return moved


def near(index, offsets, outer, inner, sign):
    steps = jnp.array(offsets, jnp.int32)
    i = lax.rem(index // inner + sign * steps[:, 0] + outer, outer)
    j = lax.rem(index % inner + sign * steps[:, 1] + inner, inner)
    return i * inner + j


def local(normed, queries, key_rows, out_grad, value_weight, doc_ids, send_to, take_from):
    dp_count = lax.axis_size("dp")
    fsdp_count = lax.axis_size("fsdp")
    planes = dp_count // 2
    side = int(fsdp_count**0.5)
    rows, depth = normed.shape
    blocks = rows // BLOCK_ROWS
    grad_scale = (rows * dp_count * fsdp_count) ** (-0.5)
    send, take = send_to[0], take_from[0]
    dp, fsdp = lax.axis_index("dp"), lax.axis_index("fsdp")
    core = dp % 2
    core_of = core.reshape(1)
    cores = [(i, i ^ 1) for i in range(dp_count)]
    dp_offsets = grid_offsets(planes, 2)
    fsdp_offsets = grid_offsets(side, side)
    number = jnp.arange(blocks, dtype=jnp.int32)

    slots = outgoing_slots(send, queries, key_rows, dp_count)
    arrived = lax.all_to_all(slots, "dp", 0, 0, tiled=True)

    width = value_weight.shape[1] // 2
    half = lax.dynamic_slice_in_dim(value_weight, core * width, width, axis=1)
    pieces = exchange([half] * fsdp_count, "fsdp", fsdp_offsets, side, side)
    own = jnp.stack(pieces)
    piece = near(fsdp, fsdp_offsets, side, side, -1)
    other = lax.ppermute(own, "dp", cores)

    target = near(dp, dp_offsets, planes, 2, 1)
    source = near(dp, dp_offsets, planes, 2, -1)
    block = jnp.sum(jnp.where(send[None, :] == target[:, None], number, 0), axis=1)
    place = jnp.sum(jnp.where(take[None, :] == source[:, None], number + 1, 0), axis=1) - 1
    leaving = value_blocks(core_of, piece, block, normed, own, other)
    landed_v = exchange(leaving, "dp", dp_offsets, planes, 2)
    packed_v = pack(place, landed_v, rows)

    column = 2 * jnp.arange(planes, dtype=jnp.int32)
    tile = depth // dp_count
    got = lax.ppermute(pick_columns(column + 1 - core, normed, tile), "dp", cores)
    turned = turn_columns(column + core, normed, got, tile)
    partner = lax.ppermute(send_to, "dp", cores)
    sends = jnp.concatenate([send_to, partner], axis=0)

    query_grad, key_grad, value_grad, returning = attention(
        take, arrived, packed_v, out_grad, doc_ids
    )
    landed = lax.all_to_all(returning, "dp", 0, 0, tiled=True)
    swapped = lax.ppermute(landed, "dp", cores)
    input_grad = input_gradient(core_of, piece, value_grad, own, other)

    chip = weight_part(sends, turned, landed, swapped, fsdp_count, planes)
    chips = lax.all_to_all(chip, "fsdp", 0, 0, tiled=True)
    plane = jnp.sum(chips.astype(jnp.float32), axis=0).astype(jnp.bfloat16)
    groups = [list(range(c, dp_count, 2)) for c in range(2)]
    parts = lax.all_to_all(plane, "dp", 0, 0, axis_index_groups=groups, tiled=True)
    weight_grad = jnp.sum(parts.astype(jnp.float32), axis=0) * grad_scale
    return (query_grad, key_grad, input_grad, weight_grad)


def solution(mesh):
    rows = P(("dp", "fsdp"), None)
    return jax.shard_map(
        local,
        mesh=mesh,
        in_specs=(rows, rows, rows, rows, P("fsdp", None), rows, rows, rows),
        out_specs=(rows, rows, rows, rows),
        check_vma=False,
    )
```

```python
import functools

import jax
import jax.numpy as jnp
from jax import lax
from jax.experimental import pallas as pl
from jax.experimental.pallas import tpu as pltpu
from jax.sharding import PartitionSpec as P


HEADS = 16
KV_HEADS = 4
HEAD_DIM = 128
GROUP = HEADS // KV_HEADS
BLOCK_ROWS = 48
QUERY_TILE = 128


def outgoing_kernel(send, q_ref, k_ref, out_ref):
    width = q_ref.shape[1]
    out_ref[0, :, :width] = q_ref[...]
    out_ref[0, :, width:] = k_ref[...]


def outgoing_slots(send, queries, key_rows, peers):
    rows, width = queries.shape
    key_width = key_rows.shape[1]
    blocks = rows // BLOCK_ROWS
    return pl.pallas_call(
        outgoing_kernel,
        grid_spec=pltpu.PrefetchScalarGridSpec(
            num_scalar_prefetch=1,
            grid=(blocks,),
            in_specs=[
                pl.BlockSpec((BLOCK_ROWS, width), lambda b, send: (b, 0)),
                pl.BlockSpec((BLOCK_ROWS, key_width), lambda b, send: (b, 0)),
            ],
            out_specs=pl.BlockSpec(
                (1, BLOCK_ROWS, width + key_width), lambda b, send: (send[b], 0, 0)
            ),
        ),
        out_shape=jax.ShapeDtypeStruct((peers, BLOCK_ROWS, width + key_width), queries.dtype),
        name="outgoing_slots",
    )(send, queries, key_rows)


def halves(core, ref, width):
    own = ref.at[:, pl.ds(pl.multiple_of(core * width, width), width)]
    other = ref.at[:, pl.ds(pl.multiple_of((1 - core) * width, width), width)]
    return own, other


def values_kernel(core, block, normed_ref, own_ref, other_ref, *rest):
    outs, total = rest[:-1], rest[-1]
    step = pl.program_id(0)
    own, other = halves(core[0], total, own_ref.shape[1])

    @pl.when(step == 0)
    def _():
        total[...] = jnp.zeros_like(total)

    rows = normed_ref[...]
    own[...] += jnp.dot(rows, own_ref[...], preferred_element_type=jnp.float32)
    other[...] += jnp.dot(rows, other_ref[...], preferred_element_type=jnp.float32)

    @pl.when(step == pl.num_programs(0) - 1)
    def _():
        for o, out in enumerate(outs):
            for c in range(out.shape[0]):
                first = pl.multiple_of(block[2 * o + c] * BLOCK_ROWS, 16)
                out[c] = total[pl.ds(first, BLOCK_ROWS), :].astype(out.dtype)


def value_blocks(core, block, normed, own, other):
    rows, depth = normed.shape
    width = own.shape[1]
    slots = block.shape[0] // 2
    tile = depth // 4
    shape = (2, BLOCK_ROWS, 2 * width)
    return pl.pallas_call(
        values_kernel,
        grid_spec=pltpu.PrefetchScalarGridSpec(
            num_scalar_prefetch=2,
            grid=(depth // tile,),
            in_specs=[
                pl.BlockSpec((rows, tile), lambda k, *_: (0, k)),
                pl.BlockSpec((tile, width), lambda k, *_: (k, 0)),
                pl.BlockSpec((tile, width), lambda k, *_: (k, 0)),
            ],
            out_specs=[pl.BlockSpec(shape, lambda k, *_: (0, 0, 0))] * slots,
            scratch_shapes=[pltpu.VMEM((rows, 2 * width), jnp.float32)],
        ),
        out_shape=[jax.ShapeDtypeStruct(shape, normed.dtype)] * slots,
        cost_estimate=pl.CostEstimate(
            flops=4 * rows * width * depth,
            bytes_accessed=2 * (normed.size + own.size + other.size),
            transcendentals=0,
        ),
        name="value_blocks",
    )(core, block, normed, own, other)


def pack_kernel(core, place, *refs):
    *own, swapped, out = refs
    sources = [ref.at[core[0]] for ref in own]
    sources += [swapped.at[o, core[0]] for o in range(swapped.shape[0])]
    for o, ref in enumerate(sources):

        @pl.when(place[o] >= 0)
        def _():
            first = pl.multiple_of(place[o] * BLOCK_ROWS, 16)
            out[pl.ds(first, BLOCK_ROWS), :] = ref[...]


def pack(core, place, own, swapped, rows):
    width = swapped.shape[3]
    shape = (2, BLOCK_ROWS, width)
    return pl.pallas_call(
        pack_kernel,
        grid_spec=pltpu.PrefetchScalarGridSpec(
            num_scalar_prefetch=2,
            grid=(1,),
            in_specs=[pl.BlockSpec(shape, lambda k, *_: (0, 0, 0))] * len(own)
            + [pl.BlockSpec((len(own),) + shape, lambda k, *_: (0, 0, 0, 0))],
            out_specs=pl.BlockSpec((rows, width), lambda k, *_: (0, 0)),
        ),
        out_shape=jax.ShapeDtypeStruct((rows, width), swapped.dtype),
    )(core, place, *own, swapped)


def turn_kernel(column, line, in_ref, *rest):
    outs, turned = rest[:-1], rest[-1]
    turned[...] = in_ref[...].T.reshape(turned.shape)
    for o, out in enumerate(outs):
        out[...] = turned[line[o]]


def turn_columns(column, line, array, tile):
    rows = array.shape[0]
    steps, lines = column.shape[0], line.shape[0]
    share = tile // lines
    return pl.pallas_call(
        turn_kernel,
        grid_spec=pltpu.PrefetchScalarGridSpec(
            num_scalar_prefetch=2,
            grid=(steps,),
            in_specs=[pl.BlockSpec((rows, tile), lambda z, column, line: (0, column[z]))],
            out_specs=[pl.BlockSpec((share, rows), lambda z, column, line: (z, 0))] * lines,
            scratch_shapes=[pltpu.VMEM((lines, share, rows), array.dtype)],
        ),
        out_shape=[jax.ShapeDtypeStruct((share * steps, rows), array.dtype)] * lines,
        name="turn_columns",
    )(column, line, array)


def input_grad_kernel(core, grad_ref, own_ref, other_ref, out_ref):
    own, other = halves(core[0], grad_ref, own_ref.shape[1])
    nt = (((1,), (1,)), ((), ()))
    total = lax.dot_general(own[...], own_ref[...], nt, preferred_element_type=jnp.float32)
    total += lax.dot_general(other[...], other_ref[...], nt, preferred_element_type=jnp.float32)
    out_ref[...] = total.astype(out_ref.dtype)


def input_gradient(core, value_grad, own, other):
    rows = value_grad.shape[0]
    depth, width = own.shape
    tile = depth // 8
    return pl.pallas_call(
        input_grad_kernel,
        grid_spec=pltpu.PrefetchScalarGridSpec(
            num_scalar_prefetch=1,
            grid=(depth // tile,),
            in_specs=[
                pl.BlockSpec((rows, 2 * width), lambda k, *_: (0, 0)),
                pl.BlockSpec((tile, width), lambda k, *_: (k, 0)),
                pl.BlockSpec((tile, width), lambda k, *_: (k, 0)),
            ],
            out_specs=pl.BlockSpec((rows, tile), lambda k, *_: (0, k)),
        ),
        out_shape=jax.ShapeDtypeStruct((rows, depth), value_grad.dtype),
        cost_estimate=pl.CostEstimate(
            flops=4 * rows * width * depth,
            bytes_accessed=2 * (rows * depth + own.size + other.size),
            transcendentals=0,
        ),
        name="input_gradient",
    )(core, value_grad, own, other)


def attention_kernel(
    take, back_block, q_ref, k_ref, v_ref, grad_ref, doc_row, doc_col,
    query_grad, key_grad, value_grad, *rest,
):
    returning = rest[:-5]
    q_rows, k_rows, bias, key_total, value_total = rest[-5:]
    rows = grad_ref.shape[0]
    blocks = rows // BLOCK_ROWS
    scale = HEAD_DIM ** (-0.5)

    @pl.when(pl.program_id(0) == 0)
    def _():
        i = lax.broadcasted_iota(jnp.int32, (rows, rows), 0)
        j = lax.broadcasted_iota(jnp.int32, (rows, rows), 1)
        allowed = (doc_col[...] == doc_row[...]) & (j <= i)
        bias[...] = jnp.where(allowed, 0.0, -jnp.inf)

    for p in range(blocks):
        place = slice(p * BLOCK_ROWS, (p + 1) * BLOCK_ROWS)
        q_rows[place, :] = q_ref[take[p]]
        k_rows[place, :] = k_ref[take[p]]

    key_total[...] = jnp.zeros_like(key_total)
    value_total[...] = jnp.zeros_like(value_total)
    for start in range(0, rows, QUERY_TILE):
        place = slice(start, start + QUERY_TILE)
        reach = start + QUERY_TILE
        q = jnp.concatenate(
            [q_rows[place, x * HEAD_DIM : (x + 1) * HEAD_DIM] for x in range(GROUP)], axis=0
        )
        g = jnp.concatenate(
            [grad_ref[place, x * HEAD_DIM : (x + 1) * HEAD_DIM] for x in range(GROUP)], axis=0
        )
        k = k_rows[:reach, :]
        v = v_ref[:reach, :]
        nt = (((1,), (1,)), ((), ()))
        tn = (((0,), (0,)), ((), ()))
        scores = lax.dot_general(q, k, nt, preferred_element_type=jnp.float32) * scale
        hide = bias[place, :reach]
        scores = scores + jnp.concatenate([hide] * GROUP, axis=0)
        peak = jnp.max(scores, axis=-1, keepdims=True)
        exponent = jnp.exp(scores - peak)
        probs = exponent / jnp.sum(exponent, axis=-1, keepdims=True)
        half = probs.astype(jnp.bfloat16)
        attn = jnp.dot(half, v, preferred_element_type=jnp.float32)
        delta = jnp.sum(g.astype(jnp.float32) * attn, axis=-1, keepdims=True)
        prob_grad = lax.dot_general(g, v, nt, preferred_element_type=jnp.float32)
        score_grad = (probs * (prob_grad - delta) * scale).astype(jnp.bfloat16)
        back = jnp.dot(score_grad, k, preferred_element_type=jnp.float32)
        for x in range(GROUP):
            query_grad[place, x * HEAD_DIM : (x + 1) * HEAD_DIM] = back[
                x * QUERY_TILE : (x + 1) * QUERY_TILE
            ].astype(query_grad.dtype)
        key_total[:reach, :] += lax.dot_general(
            score_grad, q, tn, preferred_element_type=jnp.float32
        )
        value_total[:reach, :] += lax.dot_general(half, g, tn, preferred_element_type=jnp.float32)
    key_grad[...] = key_total[...].astype(key_grad.dtype)
    value_grad[...] = value_total[...].astype(value_grad.dtype)
    for o, out in enumerate(returning):
        for c in range(out.shape[0]):
            first = pl.multiple_of(back_block[2 * o + c] * BLOCK_ROWS, 16)
            out[c] = value_total[pl.ds(first, BLOCK_ROWS), :].astype(out.dtype)


def attention(take, back_block, arrived, packed_v, out_grad, doc_ids):
    peers = arrived.shape[0]
    rows = out_grad.shape[0]
    wide = GROUP * HEAD_DIM
    first_key = HEADS
    bf16 = jnp.bfloat16
    return pl.pallas_call(
        attention_kernel,
        grid_spec=pltpu.PrefetchScalarGridSpec(
            num_scalar_prefetch=2,
            grid=(KV_HEADS,),
            in_specs=[
                pl.BlockSpec((peers, BLOCK_ROWS, wide), lambda g, *_: (0, 0, g)),
                pl.BlockSpec((peers, BLOCK_ROWS, HEAD_DIM), lambda g, *_: (0, 0, first_key + g)),
                pl.BlockSpec((rows, HEAD_DIM), lambda g, *_: (0, g)),
                pl.BlockSpec((rows, wide), lambda g, *_: (0, g)),
                pl.BlockSpec((1, rows), lambda g, *_: (0, 0)),
                pl.BlockSpec((rows, 1), lambda g, *_: (0, 0)),
            ],
            out_specs=[
                pl.BlockSpec((rows, wide), lambda g, *_: (0, g)),
                pl.BlockSpec((rows, HEAD_DIM), lambda g, *_: (0, g)),
                pl.BlockSpec((rows, HEAD_DIM), lambda g, *_: (0, g)),
            ]
            + [pl.BlockSpec((2, BLOCK_ROWS, HEAD_DIM), lambda g, *_: (0, 0, g))] * (peers // 2),
            scratch_shapes=[
                pltpu.VMEM((rows, wide), bf16),
                pltpu.VMEM((rows, HEAD_DIM), bf16),
                pltpu.VMEM((rows, rows), jnp.float32),
                pltpu.VMEM((rows, HEAD_DIM), jnp.float32),
                pltpu.VMEM((rows, HEAD_DIM), jnp.float32),
            ],
        ),
        out_shape=[
            jax.ShapeDtypeStruct((rows, KV_HEADS * wide), bf16),
            jax.ShapeDtypeStruct((rows, KV_HEADS * HEAD_DIM), bf16),
            jax.ShapeDtypeStruct((rows, KV_HEADS * HEAD_DIM), bf16),
        ]
        + [jax.ShapeDtypeStruct((2, BLOCK_ROWS, KV_HEADS * HEAD_DIM), bf16)] * (peers // 2),
        name="attention_backward",
    )(take, back_block, arrived, arrived, packed_v, out_grad, doc_ids, doc_ids.reshape(rows, 1))


def weight_kernel(loads, line, *refs):
    pieces = len(loads)
    own = pieces // 2
    sources = refs[: own + 1 + sum(loads)]
    stay, *leave = refs[len(sources) : -4]
    left, right, total, sems = refs[-4:]
    depth, rows = left.shape[1:]
    at = own + 1
    for i, parts in enumerate(loads):
        part = sources[min(i, own)].at[pl.ds(max(i - own, 0) * depth, depth)]
        pltpu.make_async_copy(part, left.at[i], sems.at[i, 0]).start()
        for j in range(parts):
            place = pl.ds(j * (rows // parts), rows // parts)
            pltpu.make_async_copy(sources[at], right.at[i, place], sems.at[i, 1]).start()
            at += 1
    total[...] = jnp.zeros_like(total)

    def add(i, _):
        pltpu.make_async_copy(left.at[i], left.at[i], sems.at[i, 0]).wait()
        pltpu.make_async_copy(right.at[i], right.at[i], sems.at[i, 1]).wait()
        part = jnp.dot(left[i], right[i], preferred_element_type=jnp.float32)
        total[...] += part.reshape(total.shape)
        return 0

    lax.fori_loop(0, pieces, add, 0)
    stay[...] = total[:, line[0]]
    for o, out in enumerate(leave):
        out[...] = total[:, line[o + 1]].astype(out.dtype)


def weight_part(line, turned, homes, steps):
    rows = turned[0].shape[1]
    depth = turned[0].shape[0] // 2
    width = homes[0][0].shape[1]
    pieces, lines = len(homes), line.shape[0]
    share = depth // steps // lines
    shape = (steps, share, width)
    loads = tuple(len(parts) for parts in homes)
    flat = [part for parts in homes for part in parts]
    bf16 = jnp.bfloat16
    return pl.pallas_call(
        functools.partial(weight_kernel, loads),
        grid_spec=pltpu.PrefetchScalarGridSpec(
            num_scalar_prefetch=1,
            grid=(1,),
            in_specs=[pl.BlockSpec(memory_space=pl.ANY)] * (len(turned) + len(flat)),
            out_specs=[pl.BlockSpec(shape, lambda k, line: (0, 0, 0))] * lines,
            scratch_shapes=[
                pltpu.VMEM((pieces, depth, rows), bf16),
                pltpu.VMEM((pieces, rows, width), bf16),
                pltpu.VMEM((steps, lines, share, width), jnp.float32),
                pltpu.SemaphoreType.DMA((pieces, 2)),
            ],
        ),
        out_shape=[jax.ShapeDtypeStruct(shape, jnp.float32)]
        + [jax.ShapeDtypeStruct(shape, bf16)] * (lines - 1),
        name="weight_part",
    )(line, *turned, *flat)


def ring(count, step, stride=1):
    size = count[1]
    return [
        (i, i + ((i // stride % size + step) % size - i // stride % size) * stride)
        for i in range(count[0])
    ]


def far_first(count):
    return sorted(range(count), key=lambda d: -min(d, count - d))


def gather_ring(array, at, size, shift):
    cut = array.shape[0] // 2
    before, after = shift(array, 1), shift(array, -1)
    top, low = shift(before[:cut], 1), shift(after[cut:], -1)
    out = jnp.zeros((size,) + array.shape, array.dtype)
    none = (0,) * (array.ndim - 1)
    for step, row, piece in ((0, 0, array), (1, 0, before), (2, 0, top), (2, cut, low), (3, 0, after)):
        out = lax.dynamic_update_slice(out, piece[None], ((at + size - step) % size, row) + none)
    return out


def local(normed, queries, key_rows, out_grad, value_weight, doc_ids, send_to, take_from):
    dp_count = lax.axis_size("dp")
    fsdp_count = lax.axis_size("fsdp")
    planes = dp_count // 2
    side = int(fsdp_count**0.5)
    rows, depth = normed.shape
    blocks = rows // BLOCK_ROWS
    grad_scale = (rows * dp_count * fsdp_count) ** (-0.5)
    send, take = send_to[0], take_from[0]
    dp, fsdp = lax.axis_index("dp"), lax.axis_index("fsdp")
    core, plane_at = dp % 2, dp // 2
    core_of = core.reshape(1)
    cores = [(i, i ^ 1) for i in range(dp_count)]
    hops = far_first(planes)
    number = jnp.arange(blocks, dtype=jnp.int32)
    hop_steps = jnp.array(hops, jnp.int32)
    pair = jnp.arange(2, dtype=jnp.int32)

    def along_z(arrays):
        return [
            a if d == 0 else lax.ppermute(a, "dp", ring((dp_count, planes), d, 2))
            for a, d in zip(arrays, hops)
        ]

    def swap(arrays):
        return [lax.ppermute(a, "dp", cores) for a in arrays]

    def along_x(array, step):
        return lax.ppermute(array, "fsdp", ring((fsdp_count, side), step, side))

    def along_y(array, step):
        return lax.ppermute(array, "fsdp", ring((fsdp_count, side), step, 1))

    def which(table, devices):
        return jnp.sum(jnp.where(table[None, :] == devices[:, None], number + 1, 0), axis=1) - 1

    slots = outgoing_slots(send, queries, key_rows, dp_count)
    arrived = lax.all_to_all(slots, "dp", 0, 0, tiled=True)

    width = value_weight.shape[1] // 2
    half = lax.dynamic_slice_in_dim(value_weight, core * width, width, axis=1)
    x, y = fsdp // side, fsdp % side
    line = gather_ring(half, x, side, along_x)
    own = gather_ring(line, y, side, along_y)
    own = jnp.transpose(own, (1, 0, 2, 3)).reshape(depth, width)
    (other,) = swap([own])

    onward = (((plane_at + hop_steps) % planes * 2)[:, None] + pair).reshape(-1)
    origin = (plane_at + planes - hop_steps) % planes * 2
    origin = jnp.concatenate([origin + core, origin + 1 - core])
    block = jnp.maximum(which(send, onward), 0)
    back_block = jnp.maximum(which(take, onward), 0)
    place, home_place = which(take, origin), which(send, origin)
    leaving = value_blocks(core_of, block, normed, own, other)
    landed = along_z(leaving)
    (swapped,) = swap([jnp.stack(landed)])
    packed_v = pack(core_of, place, landed, swapped, rows)

    column = 2 * jnp.arange(planes, dtype=jnp.int32)
    tile = depth // dp_count
    x_line = (x + jnp.arange(side, dtype=jnp.int32)) % side
    columns = jnp.concatenate([column + core, column + 1 - core])
    turned = turn_columns(columns, x_line, normed, tile)
    turned = [along_x(a, d) if d else a for d, a in enumerate(turned)]

    query_grad, key_grad, value_grad, *returning = attention(
        take, back_block, arrived, packed_v, out_grad, doc_ids
    )
    landed = along_z(returning)
    (swapped,) = swap([jnp.stack(landed)])
    home = pack(core_of, home_place, landed, swapped, rows)
    cut = rows // 2
    before, after = along_x(home, 1), along_x(home, -1)
    top, low = along_x(before[:cut], 1), along_x(after[cut:], -1)
    homes = [(home,), (before,), (top, low), (after,)]
    homes += [tuple(swap(parts)) for parts in homes]
    theirs = jnp.concatenate([a[a.shape[0] // 2 :] for a in turned])
    turned += swap([theirs])

    y_line = (y + jnp.arange(side, dtype=jnp.int32)) % side
    stay, *leave = weight_part(y_line, turned, homes, planes)
    leave = [along_y(a, d + 1) for d, a in enumerate(leave)]
    plane = (stay + sum(a.astype(jnp.float32) for a in leave)).astype(jnp.bfloat16)
    groups = [list(range(c, dp_count, 2)) for c in range(2)]
    parts = lax.all_to_all(plane, "dp", 0, 0, axis_index_groups=groups, tiled=True)
    input_grad = input_gradient(core_of, value_grad, own, other)
    weight_grad = jnp.sum(parts.astype(jnp.float32), axis=0) * grad_scale
    return (query_grad, key_grad, input_grad, weight_grad)


def solution(mesh):
    rows = P(("dp", "fsdp"), None)
    return jax.shard_map(
        local,
        mesh=mesh,
        in_specs=(rows, rows, rows, rows, P("fsdp", None), rows, rows, rows),
        out_specs=(rows, rows, rows, rows),
        check_vma=False,
    )
```

```python
import jax
import jax.numpy as jnp
from jax import lax
from jax.experimental import pallas as pl
from jax.experimental.pallas import tpu as pltpu
from jax.sharding import PartitionSpec as P


HEADS = 16
KV_HEADS = 4
HEAD_DIM = 128
GROUP = HEADS // KV_HEADS
BLOCK_ROWS = 48
QUERY_TILE = 128


def outgoing_kernel(send, *refs):
    *sources, out = refs
    at = 0
    for ref in sources:
        out[0, :, at : at + ref.shape[1]] = ref[...]
        at += ref.shape[1]


def outgoing_slots(send, sources, peers):
    blocks = send.shape[0]
    width = sum(columns for _, columns, _ in sources)
    dtype = sources[0][0].dtype
    return pl.pallas_call(
        outgoing_kernel,
        grid_spec=pltpu.PrefetchScalarGridSpec(
            num_scalar_prefetch=1,
            grid=(blocks,),
            in_specs=[
                pl.BlockSpec((BLOCK_ROWS, columns), lambda b, send, at=at: (b, at))
                for _, columns, at in sources
            ],
            out_specs=pl.BlockSpec((1, BLOCK_ROWS, width), lambda b, send: (send[b], 0, 0)),
        ),
        out_shape=jax.ShapeDtypeStruct((peers, BLOCK_ROWS, width), dtype),
        name="outgoing_slots",
    )(send, *(array for array, _, _ in sources))


def halves(core, ref, width):
    own = ref.at[:, pl.ds(pl.multiple_of(core * width, width), width)]
    other = ref.at[:, pl.ds(pl.multiple_of((1 - core) * width, width), width)]
    return own, other


def values_kernel(core, block, normed_ref, own_ref, other_ref, *rest):
    outs, total = rest[:-1], rest[-1]
    step = pl.program_id(0)
    own, other = halves(core[0], total, own_ref.shape[1])

    @pl.when(step == 0)
    def _():
        total[...] = jnp.zeros_like(total)

    rows = normed_ref[...]
    own[...] += jnp.dot(rows, own_ref[...], preferred_element_type=jnp.float32)
    other[...] += jnp.dot(rows, other_ref[...], preferred_element_type=jnp.float32)

    @pl.when(step == pl.num_programs(0) - 1)
    def _():
        for o, out in enumerate(outs):
            for c in range(out.shape[0]):
                first = pl.multiple_of(block[2 * o + c] * BLOCK_ROWS, 16)
                out[c] = total[pl.ds(first, BLOCK_ROWS), :].astype(out.dtype)


def value_blocks(core, block, normed, own, other):
    rows, depth = normed.shape
    width = own.shape[1]
    slots = block.shape[0] // 2
    tile = depth // 4
    shape = (2, BLOCK_ROWS, 2 * width)
    return pl.pallas_call(
        values_kernel,
        grid_spec=pltpu.PrefetchScalarGridSpec(
            num_scalar_prefetch=2,
            grid=(depth // tile,),
            in_specs=[
                pl.BlockSpec((rows, tile), lambda k, *_: (0, k)),
                pl.BlockSpec((tile, width), lambda k, *_: (k, 0)),
                pl.BlockSpec((tile, width), lambda k, *_: (k, 0)),
            ],
            out_specs=[pl.BlockSpec(shape, lambda k, *_: (0, 0, 0))] * slots,
            scratch_shapes=[pltpu.VMEM((rows, 2 * width), jnp.float32)],
        ),
        out_shape=[jax.ShapeDtypeStruct(shape, normed.dtype)] * slots,
        cost_estimate=pl.CostEstimate(
            flops=4 * rows * width * depth,
            bytes_accessed=2 * (normed.size + own.size + other.size),
            transcendentals=0,
        ),
        name="value_blocks",
    )(core, block, normed, own, other)


def pack_kernel(core, place, *refs):
    *own, swapped, out = refs
    sources = [ref.at[core[0]] for ref in own]
    sources += [swapped.at[o, core[0]] for o in range(swapped.shape[0])]
    for o, ref in enumerate(sources):

        @pl.when(place[o] >= 0)
        def _():
            first = pl.multiple_of(place[o] * BLOCK_ROWS, 16)
            out[pl.ds(first, BLOCK_ROWS), :] = ref[...]


def pack(core, place, own, swapped, rows):
    width = swapped.shape[3]
    shape = (2, BLOCK_ROWS, width)
    return pl.pallas_call(
        pack_kernel,
        grid_spec=pltpu.PrefetchScalarGridSpec(
            num_scalar_prefetch=2,
            grid=(1,),
            in_specs=[pl.BlockSpec(shape, lambda k, *_: (0, 0, 0))] * len(own)
            + [pl.BlockSpec((len(own),) + shape, lambda k, *_: (0, 0, 0, 0))],
            out_specs=pl.BlockSpec((rows, width), lambda k, *_: (0, 0)),
        ),
        out_shape=jax.ShapeDtypeStruct((rows, width), swapped.dtype),
    )(core, place, *own, swapped)


def pick_kernel(column, in_ref, out_ref):
    out_ref[...] = in_ref[...]


def pick_columns(column, array, tile):
    rows = array.shape[0]
    steps = column.shape[0]
    return pl.pallas_call(
        pick_kernel,
        grid_spec=pltpu.PrefetchScalarGridSpec(
            num_scalar_prefetch=1,
            grid=(steps,),
            in_specs=[pl.BlockSpec((rows, tile), lambda z, column: (0, column[z]))],
            out_specs=pl.BlockSpec((rows, tile), lambda z, column: (0, z)),
        ),
        out_shape=jax.ShapeDtypeStruct((rows, tile * steps), array.dtype),
        name="pick_columns",
    )(column, array)


def turn_kernel(column, own_ref, got_ref, out_ref):
    rows = own_ref.shape[0]
    out_ref[:, :rows] = own_ref[...].T
    out_ref[:, rows:] = got_ref[...].T


def turn_columns(column, array, got, tile):
    rows = array.shape[0]
    steps = column.shape[0]
    return pl.pallas_call(
        turn_kernel,
        grid_spec=pltpu.PrefetchScalarGridSpec(
            num_scalar_prefetch=1,
            grid=(steps,),
            in_specs=[
                pl.BlockSpec((rows, tile), lambda z, column: (0, column[z])),
                pl.BlockSpec((rows, tile), lambda z, column: (0, z)),
            ],
            out_specs=pl.BlockSpec((tile, 2 * rows), lambda z, column: (z, 0)),
        ),
        out_shape=jax.ShapeDtypeStruct((tile * steps, 2 * rows), array.dtype),
        name="turn_columns",
    )(column, array, got)


def input_grad_kernel(core, grad_ref, own_ref, other_ref, out_ref):
    own, other = halves(core[0], grad_ref, own_ref.shape[1])
    nt = (((1,), (1,)), ((), ()))
    total = lax.dot_general(own[...], own_ref[...], nt, preferred_element_type=jnp.float32)
    total += lax.dot_general(other[...], other_ref[...], nt, preferred_element_type=jnp.float32)
    out_ref[...] = total.astype(out_ref.dtype)


def input_gradient(core, value_grad, own, other):
    rows = value_grad.shape[0]
    depth, width = own.shape
    tile = depth // 8
    return pl.pallas_call(
        input_grad_kernel,
        grid_spec=pltpu.PrefetchScalarGridSpec(
            num_scalar_prefetch=1,
            grid=(depth // tile,),
            in_specs=[
                pl.BlockSpec((rows, 2 * width), lambda k, *_: (0, 0)),
                pl.BlockSpec((tile, width), lambda k, *_: (k, 0)),
                pl.BlockSpec((tile, width), lambda k, *_: (k, 0)),
            ],
            out_specs=pl.BlockSpec((rows, tile), lambda k, *_: (0, k)),
        ),
        out_shape=jax.ShapeDtypeStruct((rows, depth), value_grad.dtype),
        cost_estimate=pl.CostEstimate(
            flops=4 * rows * width * depth,
            bytes_accessed=2 * (rows * depth + own.size + other.size),
            transcendentals=0,
        ),
        name="input_gradient",
    )(core, value_grad, own, other)


def attention_kernel(take, q_ref, k_ref, v_ref, grad_ref, doc_row, doc_col, *rest):
    query_grad, key_grad, value_grad, returning = rest[-9:-5]
    q_rows, k_rows, bias, key_total, value_total = rest[-5:]
    rows = grad_ref.shape[0]
    blocks = rows // BLOCK_ROWS
    scale = HEAD_DIM ** (-0.5)

    @pl.when(pl.program_id(0) == 0)
    def _():
        i = lax.broadcasted_iota(jnp.int32, (rows, rows), 0)
        j = lax.broadcasted_iota(jnp.int32, (rows, rows), 1)
        allowed = (doc_col[...] == doc_row[...]) & (j <= i)
        bias[...] = jnp.where(allowed, 0.0, -jnp.inf)

    for p in range(blocks):
        place = slice(p * BLOCK_ROWS, (p + 1) * BLOCK_ROWS)
        q_rows[place, :] = q_ref[take[p]]
        k_rows[place, :] = k_ref[take[p]]

    key_total[...] = jnp.zeros_like(key_total)
    value_total[...] = jnp.zeros_like(value_total)
    for start in range(0, rows, QUERY_TILE):
        place = slice(start, start + QUERY_TILE)
        reach = start + QUERY_TILE
        q = jnp.concatenate(
            [q_rows[place, x * HEAD_DIM : (x + 1) * HEAD_DIM] for x in range(GROUP)], axis=0
        )
        g = jnp.concatenate(
            [grad_ref[place, x * HEAD_DIM : (x + 1) * HEAD_DIM] for x in range(GROUP)], axis=0
        )
        k = k_rows[:reach, :]
        v = v_ref[:reach, :]
        nt = (((1,), (1,)), ((), ()))
        tn = (((0,), (0,)), ((), ()))
        scores = lax.dot_general(q, k, nt, preferred_element_type=jnp.float32) * scale
        hide = bias[place, :reach]
        scores = scores + jnp.concatenate([hide] * GROUP, axis=0)
        peak = jnp.max(scores, axis=-1, keepdims=True)
        exponent = jnp.exp(scores - peak)
        probs = exponent / jnp.sum(exponent, axis=-1, keepdims=True)
        half = probs.astype(jnp.bfloat16)
        attn = jnp.dot(half, v, preferred_element_type=jnp.float32)
        delta = jnp.sum(g.astype(jnp.float32) * attn, axis=-1, keepdims=True)
        prob_grad = lax.dot_general(g, v, nt, preferred_element_type=jnp.float32)
        score_grad = (probs * (prob_grad - delta) * scale).astype(jnp.bfloat16)
        back = jnp.dot(score_grad, k, preferred_element_type=jnp.float32)
        for x in range(GROUP):
            query_grad[place, x * HEAD_DIM : (x + 1) * HEAD_DIM] = back[
                x * QUERY_TILE : (x + 1) * QUERY_TILE
            ].astype(query_grad.dtype)
        key_total[:reach, :] += lax.dot_general(
            score_grad, q, tn, preferred_element_type=jnp.float32
        )
        value_total[:reach, :] += lax.dot_general(half, g, tn, preferred_element_type=jnp.float32)
    key_grad[...] = key_total[...].astype(key_grad.dtype)
    value_grad[...] = value_total[...].astype(value_grad.dtype)
    returning[...] = jnp.zeros_like(returning)
    for p in range(blocks):
        place = slice(p * BLOCK_ROWS, (p + 1) * BLOCK_ROWS)
        returning[take[p]] = value_total[place, :].astype(returning.dtype)


def attention(take, arrived_q, arrived_k, packed_v, out_grad, doc_ids, first, count, key_at, done):
    peers = arrived_q.shape[0]
    rows = out_grad.shape[0]
    wide = GROUP * HEAD_DIM
    bf16 = jnp.bfloat16
    slot = (peers, BLOCK_ROWS, HEAD_DIM)
    return pl.pallas_call(
        attention_kernel,
        grid_spec=pltpu.PrefetchScalarGridSpec(
            num_scalar_prefetch=1,
            grid=(count,),
            in_specs=[
                pl.BlockSpec((peers, BLOCK_ROWS, wide), lambda g, take: (0, 0, g)),
                pl.BlockSpec(slot, lambda g, take: (0, 0, key_at + first + g)),
                pl.BlockSpec((rows, HEAD_DIM), lambda g, take: (0, first + g)),
                pl.BlockSpec((rows, wide), lambda g, take: (0, first + g)),
                pl.BlockSpec((1, rows), lambda g, take: (0, 0)),
                pl.BlockSpec((rows, 1), lambda g, take: (0, 0)),
            ]
            + [pl.BlockSpec(memory_space=pl.ANY)] * len(done),
            out_specs=[
                pl.BlockSpec((rows, wide), lambda g, take: (0, first + g)),
                pl.BlockSpec((rows, HEAD_DIM), lambda g, take: (0, first + g)),
                pl.BlockSpec((rows, HEAD_DIM), lambda g, take: (0, first + g)),
                pl.BlockSpec(slot, lambda g, take: (0, 0, first + g)),
            ],
            scratch_shapes=[
                pltpu.VMEM((rows, wide), bf16),
                pltpu.VMEM((rows, HEAD_DIM), bf16),
                pltpu.VMEM((rows, rows), jnp.float32),
                pltpu.VMEM((rows, HEAD_DIM), jnp.float32),
                pltpu.VMEM((rows, HEAD_DIM), jnp.float32),
            ],
        ),
        out_shape=[
            jax.ShapeDtypeStruct((rows, KV_HEADS * wide), bf16),
            jax.ShapeDtypeStruct((rows, KV_HEADS * HEAD_DIM), bf16),
            jax.ShapeDtypeStruct((rows, KV_HEADS * HEAD_DIM), bf16),
            jax.ShapeDtypeStruct((peers, BLOCK_ROWS, KV_HEADS * HEAD_DIM), bf16),
        ],
        input_output_aliases={7 + i: i for i in range(len(done))},
        cost_estimate=pl.CostEstimate(
            flops=12 * rows * rows * HEAD_DIM * GROUP * count,
            bytes_accessed=10 * rows * wide * count,
            transcendentals=rows * rows * GROUP * count,
        ),
        name="attention_backward",
    )(take, arrived_q, arrived_k, packed_v, out_grad, doc_ids, doc_ids.reshape(rows, 1), *done)


def weight_kernel(send, turned_ref, landed_ref, swapped_ref, out_ref, home):
    rows = home.shape[0] // 2

    @pl.when(pl.program_id(0) == 0)
    def _():
        for b in range(rows // BLOCK_ROWS):
            place = slice(b * BLOCK_ROWS, (b + 1) * BLOCK_ROWS)
            home[place, :] = landed_ref[send[0, b]]
        for b in range(rows // BLOCK_ROWS):
            place = slice(rows + b * BLOCK_ROWS, rows + (b + 1) * BLOCK_ROWS)
            home[place, :] = swapped_ref[send[1, b]]

    part = jnp.dot(turned_ref[...], home[...], preferred_element_type=jnp.float32)
    columns, share, inner, width = out_ref.shape
    part = part.reshape(share, columns, inner, width).astype(out_ref.dtype)
    for i in range(share):
        out_ref[:, i] = part[i]


def weight_part(send, turned, landed, swapped, columns, steps):
    depth, rows = turned.shape
    peers, _, width = landed.shape
    inner = depth // steps // columns
    share = 4
    tile = share * inner * columns
    return pl.pallas_call(
        weight_kernel,
        grid_spec=pltpu.PrefetchScalarGridSpec(
            num_scalar_prefetch=1,
            grid=(steps // share,),
            in_specs=[
                pl.BlockSpec((tile, rows), lambda z, send: (z, 0)),
                pl.BlockSpec((peers, BLOCK_ROWS, width), lambda z, send: (0, 0, 0)),
                pl.BlockSpec((peers, BLOCK_ROWS, width), lambda z, send: (0, 0, 0)),
            ],
            out_specs=pl.BlockSpec((columns, share, inner, width), lambda z, send: (0, z, 0, 0)),
            scratch_shapes=[pltpu.VMEM((rows, width), jnp.bfloat16)],
        ),
        out_shape=jax.ShapeDtypeStruct((columns, steps, inner, width), jnp.bfloat16),
        name="weight_part",
    )(send, turned, landed, swapped)


def ring(count, step, stride=1):
    size = count[1]
    return [
        (i, i + ((i // stride % size + step) % size - i // stride % size) * stride)
        for i in range(count[0])
    ]


def far_first(count):
    return sorted(range(count), key=lambda d: -min(d, count - d))


def gather_ring(array, at, size, shift):
    cut = array.shape[0] // 2
    before, after = shift(array, 1), shift(array, -1)
    top, low = shift(before[:cut], 1), shift(after[cut:], -1)
    out = jnp.zeros((size,) + array.shape, array.dtype)
    none = (0,) * (array.ndim - 1)
    for step, row, piece in ((0, 0, array), (1, 0, before), (2, 0, top), (2, cut, low), (3, 0, after)):
        out = lax.dynamic_update_slice(out, piece[None], ((at + size - step) % size, row) + none)
    return out


def local(normed, queries, key_rows, out_grad, value_weight, doc_ids, send_to, take_from):
    dp_count = lax.axis_size("dp")
    fsdp_count = lax.axis_size("fsdp")
    planes = dp_count // 2
    side = int(fsdp_count**0.5)
    rows, depth = normed.shape
    blocks = rows // BLOCK_ROWS
    grad_scale = (rows * dp_count * fsdp_count) ** (-0.5)
    send, take = send_to[0], take_from[0]
    dp, fsdp = lax.axis_index("dp"), lax.axis_index("fsdp")
    core, plane_at = dp % 2, dp // 2
    core_of = core.reshape(1)
    cores = [(i, i ^ 1) for i in range(dp_count)]
    hops = far_first(planes)
    number = jnp.arange(blocks, dtype=jnp.int32)
    hop_steps = jnp.array(hops, jnp.int32)
    pair = jnp.arange(2, dtype=jnp.int32)

    def along_z(arrays):
        return [
            a if d == 0 else lax.ppermute(a, "dp", ring((dp_count, planes), d, 2))
            for a, d in zip(arrays, hops)
        ]

    def swap(arrays):
        return [lax.ppermute(a, "dp", cores) for a in arrays]

    def along_x(array, step):
        return lax.ppermute(array, "fsdp", ring((fsdp_count, side), step, side))

    def along_y(array, step):
        return lax.ppermute(array, "fsdp", ring((fsdp_count, side), step, 1))

    def which(table, devices):
        return jnp.sum(jnp.where(table[None, :] == devices[:, None], number + 1, 0), axis=1) - 1

    wide = queries.shape[1] // 2
    keys = key_rows.shape[1]
    slots = outgoing_slots(send, [(queries, wide, 0), (key_rows, keys, 0)], dp_count)
    arrived_one = lax.all_to_all(slots, "dp", 0, 0, tiled=True)
    slots = outgoing_slots(send, [(queries, wide, 1)], dp_count)
    arrived_two = lax.all_to_all(slots, "dp", 0, 0, tiled=True)

    width = value_weight.shape[1] // 2
    half = lax.dynamic_slice_in_dim(value_weight, core * width, width, axis=1)
    x, y = fsdp // side, fsdp % side
    line = gather_ring(half, x, side, along_x)
    own = gather_ring(line, y, side, along_y)
    own = jnp.transpose(own, (1, 0, 2, 3)).reshape(depth, width)
    (other,) = swap([own])

    onward = (((plane_at + hop_steps) % planes * 2)[:, None] + pair).reshape(-1)
    origin = (plane_at + planes - hop_steps) % planes * 2
    origin = jnp.concatenate([origin + core, origin + 1 - core])
    block = jnp.maximum(which(send, onward), 0)
    place = which(take, origin)
    leaving = value_blocks(core_of, block, normed, own, other)
    landed = along_z(leaving)
    (swapped,) = swap([jnp.stack(landed)])
    packed_v = pack(core_of, place, landed, swapped, rows)

    column = 2 * jnp.arange(planes, dtype=jnp.int32)
    tile = depth // dp_count
    picked = pick_columns(column + 1 - core, normed, tile)
    (got,) = swap([picked])
    turned = turn_columns(column + core, normed, got, tile)
    (partner,) = swap([send_to])
    sends = jnp.concatenate([send_to, partner], axis=0)

    half_groups = KV_HEADS // 2
    key_at = wide // HEAD_DIM
    done = attention(
        take, arrived_one, arrived_one, packed_v, out_grad, doc_ids,
        0, half_groups, key_at, (),
    )
    query_grad, key_grad, value_grad, returning = attention(
        take, arrived_two, arrived_one, packed_v, out_grad, doc_ids,
        half_groups, half_groups, key_at, done,
    )
    landed = lax.all_to_all(returning, "dp", 0, 0, tiled=True)
    (swapped,) = swap([landed])
    input_grad = input_gradient(core_of, value_grad, own, other)

    chip = weight_part(sends, turned, landed, swapped, fsdp_count, planes)
    chips = lax.all_to_all(chip, "fsdp", 0, 0, tiled=True)
    plane = jnp.sum(chips.astype(jnp.float32), axis=0).astype(jnp.bfloat16)
    groups = [list(range(c, dp_count, 2)) for c in range(2)]
    parts = lax.all_to_all(plane, "dp", 0, 0, axis_index_groups=groups, tiled=True)
    weight_grad = jnp.sum(parts.astype(jnp.float32), axis=0) * grad_scale
    return (query_grad, key_grad, input_grad, weight_grad)


def solution(mesh):
    rows = P(("dp", "fsdp"), None)
    return jax.shard_map(
        local,
        mesh=mesh,
        in_specs=(rows, rows, rows, rows, P("fsdp", None), rows, rows, rows),
        out_specs=(rows, rows, rows, rows),
        check_vma=False,
    )
```

```python
import functools

import jax
import jax.numpy as jnp
from jax import lax
from jax.experimental import pallas as pl
from jax.experimental.pallas import tpu as pltpu
from jax.sharding import PartitionSpec as P


HEADS = 16
KV_HEADS = 4
HEAD_DIM = 128
GROUP = HEADS // KV_HEADS
BLOCK_ROWS = 48
QUERY_TILE = 128


def outgoing_kernel(send, *refs):
    *sources, out = refs
    at = 0
    for ref in sources:
        out[0, :, at : at + ref.shape[1]] = ref[...]
        at += ref.shape[1]


def outgoing_slots(send, sources, peers):
    blocks = send.shape[0]
    width = sum(columns for _, columns, _ in sources)
    dtype = sources[0][0].dtype
    return pl.pallas_call(
        outgoing_kernel,
        grid_spec=pltpu.PrefetchScalarGridSpec(
            num_scalar_prefetch=1,
            grid=(blocks,),
            in_specs=[
                pl.BlockSpec((BLOCK_ROWS, columns), lambda b, send, at=at: (b, at))
                for _, columns, at in sources
            ],
            out_specs=pl.BlockSpec((1, BLOCK_ROWS, width), lambda b, send: (send[b], 0, 0)),
        ),
        out_shape=jax.ShapeDtypeStruct((peers, BLOCK_ROWS, width), dtype),
        name="outgoing_slots",
    )(send, *(array for array, _, _ in sources))


def halves(core, ref, width):
    own = ref.at[:, pl.ds(pl.multiple_of(core * width, width), width)]
    other = ref.at[:, pl.ds(pl.multiple_of((1 - core) * width, width), width)]
    return own, other


def values_kernel(core, block, normed_ref, own_ref, other_ref, *rest):
    outs, total = rest[:-1], rest[-1]
    step = pl.program_id(0)
    own, other = halves(core[0], total, own_ref.shape[1])

    @pl.when(step == 0)
    def _():
        total[...] = jnp.zeros_like(total)

    rows = normed_ref[...]
    own[...] += jnp.dot(rows, own_ref[...], preferred_element_type=jnp.float32)
    other[...] += jnp.dot(rows, other_ref[...], preferred_element_type=jnp.float32)

    @pl.when(step == pl.num_programs(0) - 1)
    def _():
        for o, out in enumerate(outs):
            for c in range(out.shape[0]):
                first = pl.multiple_of(block[2 * o + c] * BLOCK_ROWS, 16)
                out[c] = total[pl.ds(first, BLOCK_ROWS), :].astype(out.dtype)


def value_blocks(core, block, normed, own, other):
    rows, depth = normed.shape
    width = own.shape[1]
    slots = block.shape[0] // 2
    tile = depth // 4
    shape = (2, BLOCK_ROWS, 2 * width)
    return pl.pallas_call(
        values_kernel,
        grid_spec=pltpu.PrefetchScalarGridSpec(
            num_scalar_prefetch=2,
            grid=(depth // tile,),
            in_specs=[
                pl.BlockSpec((rows, tile), lambda k, *_: (0, k)),
                pl.BlockSpec((tile, width), lambda k, *_: (k, 0)),
                pl.BlockSpec((tile, width), lambda k, *_: (k, 0)),
            ],
            out_specs=[pl.BlockSpec(shape, lambda k, *_: (0, 0, 0))] * slots,
            scratch_shapes=[pltpu.VMEM((rows, 2 * width), jnp.float32)],
        ),
        out_shape=[jax.ShapeDtypeStruct(shape, normed.dtype)] * slots,
        cost_estimate=pl.CostEstimate(
            flops=4 * rows * width * depth,
            bytes_accessed=2 * (normed.size + own.size + other.size),
            transcendentals=0,
        ),
        name="value_blocks",
    )(core, block, normed, own, other)


def pack_kernel(core, place, *refs):
    out = refs[-1]
    *own, swapped = refs[:-1]
    sources = [ref.at[core[0]] for ref in own] + [swapped.at[o] for o in range(swapped.shape[0])]
    for o, ref in enumerate(sources):

        @pl.when(place[o] >= 0)
        def _():
            first = pl.multiple_of(place[o] * BLOCK_ROWS, 16)
            out[pl.ds(first, BLOCK_ROWS), :] = ref[...]


def pack(core, place, own, swapped, rows):
    width = swapped.shape[2]
    shape = (2, BLOCK_ROWS, width)
    return pl.pallas_call(
        pack_kernel,
        grid_spec=pltpu.PrefetchScalarGridSpec(
            num_scalar_prefetch=2,
            grid=(1,),
            in_specs=[pl.BlockSpec(shape, lambda k, *_: (0, 0, 0))] * len(own)
            + [pl.BlockSpec(swapped.shape, lambda k, *_: (0, 0, 0))],
            out_specs=pl.BlockSpec((rows, width), lambda k, *_: (0, 0)),
        ),
        out_shape=jax.ShapeDtypeStruct((rows, width), swapped.dtype),
        name="pack_values",
    )(core, place, *own, swapped)


def pick_kernel(column, in_ref, out_ref):
    out_ref[...] = in_ref[...]


def pick_columns(column, array, tile):
    rows = array.shape[0]
    steps = column.shape[0]
    return pl.pallas_call(
        pick_kernel,
        grid_spec=pltpu.PrefetchScalarGridSpec(
            num_scalar_prefetch=1,
            grid=(steps,),
            in_specs=[pl.BlockSpec((rows, tile), lambda z, column: (0, column[z]))],
            out_specs=pl.BlockSpec((rows, tile), lambda z, column: (0, z)),
        ),
        out_shape=jax.ShapeDtypeStruct((rows, tile * steps), array.dtype),
        name="pick_columns",
    )(column, array)


def turn_kernel(column, own_ref, got_ref, out_ref):
    rows = own_ref.shape[0]
    out_ref[:, :rows] = own_ref[...].T
    out_ref[:, rows:] = got_ref[...].T


def turn_columns(column, array, got, tile):
    rows = array.shape[0]
    steps = column.shape[0]
    return pl.pallas_call(
        turn_kernel,
        grid_spec=pltpu.PrefetchScalarGridSpec(
            num_scalar_prefetch=1,
            grid=(steps,),
            in_specs=[
                pl.BlockSpec((rows, tile), lambda z, column: (0, column[z])),
                pl.BlockSpec((rows, tile), lambda z, column: (0, z)),
            ],
            out_specs=pl.BlockSpec((tile, 2 * rows), lambda z, column: (z, 0)),
        ),
        out_shape=jax.ShapeDtypeStruct((tile * steps, 2 * rows), array.dtype),
        name="turn_columns",
    )(column, array, got)


def input_grad_kernel(core, grad_ref, own_ref, other_ref, out_ref):
    own, other = halves(core[0], grad_ref, own_ref.shape[1])
    nt = (((1,), (1,)), ((), ()))
    total = lax.dot_general(own[...], own_ref[...], nt, preferred_element_type=jnp.float32)
    total += lax.dot_general(other[...], other_ref[...], nt, preferred_element_type=jnp.float32)
    out_ref[...] = total.astype(out_ref.dtype)


def input_gradient(core, value_grad, own, other):
    rows = value_grad.shape[0]
    depth, width = own.shape
    tile = depth // 8
    return pl.pallas_call(
        input_grad_kernel,
        grid_spec=pltpu.PrefetchScalarGridSpec(
            num_scalar_prefetch=1,
            grid=(depth // tile,),
            in_specs=[
                pl.BlockSpec((rows, 2 * width), lambda k, *_: (0, 0)),
                pl.BlockSpec((tile, width), lambda k, *_: (k, 0)),
                pl.BlockSpec((tile, width), lambda k, *_: (k, 0)),
            ],
            out_specs=pl.BlockSpec((rows, tile), lambda k, *_: (0, k)),
        ),
        out_shape=jax.ShapeDtypeStruct((rows, depth), value_grad.dtype),
        cost_estimate=pl.CostEstimate(
            flops=4 * rows * width * depth,
            bytes_accessed=2 * (rows * depth + own.size + other.size),
            transcendentals=0,
        ),
        name="input_gradient",
    )(core, value_grad, own, other)


def attention_kernel(kept, take, back_block, q_ref, k_ref, v_ref, grad_ref, doc_row, doc_col, *rest):
    query_grad, key_grad, value_grad, *returning = rest[kept:-5]
    q_rows, k_rows, bias, key_total, value_total = rest[-5:]
    rows = grad_ref.shape[0]
    blocks = rows // BLOCK_ROWS
    scale = HEAD_DIM ** (-0.5)

    @pl.when(pl.program_id(0) == 0)
    def _():
        i = lax.broadcasted_iota(jnp.int32, (rows, rows), 0)
        j = lax.broadcasted_iota(jnp.int32, (rows, rows), 1)
        allowed = (doc_col[...] == doc_row[...]) & (j <= i)
        bias[...] = jnp.where(allowed, 0.0, -jnp.inf)

    for p in range(blocks):
        place = slice(p * BLOCK_ROWS, (p + 1) * BLOCK_ROWS)
        q_rows[place, :] = q_ref[take[p]]
        k_rows[place, :] = k_ref[take[p]]

    key_total[...] = jnp.zeros_like(key_total)
    value_total[...] = jnp.zeros_like(value_total)
    for start in range(0, rows, QUERY_TILE):
        place = slice(start, start + QUERY_TILE)
        reach = start + QUERY_TILE
        q = jnp.concatenate(
            [q_rows[place, x * HEAD_DIM : (x + 1) * HEAD_DIM] for x in range(GROUP)], axis=0
        )
        g = jnp.concatenate(
            [grad_ref[place, x * HEAD_DIM : (x + 1) * HEAD_DIM] for x in range(GROUP)], axis=0
        )
        k = k_rows[:reach, :]
        v = v_ref[:reach, :]
        nt = (((1,), (1,)), ((), ()))
        tn = (((0,), (0,)), ((), ()))
        scores = lax.dot_general(q, k, nt, preferred_element_type=jnp.float32) * scale
        hide = bias[place, :reach]
        scores = scores + jnp.concatenate([hide] * GROUP, axis=0)
        peak = jnp.max(scores, axis=-1, keepdims=True)
        exponent = jnp.exp(scores - peak)
        probs = exponent / jnp.sum(exponent, axis=-1, keepdims=True)
        half = probs.astype(jnp.bfloat16)
        attn = jnp.dot(half, v, preferred_element_type=jnp.float32)
        delta = jnp.sum(g.astype(jnp.float32) * attn, axis=-1, keepdims=True)
        prob_grad = lax.dot_general(g, v, nt, preferred_element_type=jnp.float32)
        score_grad = (probs * (prob_grad - delta) * scale).astype(jnp.bfloat16)
        back = jnp.dot(score_grad, k, preferred_element_type=jnp.float32)
        for x in range(GROUP):
            query_grad[place, x * HEAD_DIM : (x + 1) * HEAD_DIM] = back[
                x * QUERY_TILE : (x + 1) * QUERY_TILE
            ].astype(query_grad.dtype)
        key_total[:reach, :] += lax.dot_general(
            score_grad, q, tn, preferred_element_type=jnp.float32
        )
        value_total[:reach, :] += lax.dot_general(half, g, tn, preferred_element_type=jnp.float32)
    key_grad[...] = key_total[...].astype(key_grad.dtype)
    value_grad[...] = value_total[...].astype(value_grad.dtype)
    if len(returning) > 1:
        for o, out in enumerate(returning):
            for c in range(out.shape[0]):
                first = pl.multiple_of(back_block[2 * o + c] * BLOCK_ROWS, 16)
                out[c] = value_total[pl.ds(first, BLOCK_ROWS), :].astype(out.dtype)
    else:
        for p in range(blocks):
            place = slice(p * BLOCK_ROWS, (p + 1) * BLOCK_ROWS)
            returning[0][take[p]] = value_total[place, :].astype(returning[0].dtype)


def attention(
    take, back, arrived_q, arrived_k, packed_v, out_grad, doc_ids, first, count, key_at, done, parts
):
    peers = arrived_q.shape[0]
    rows = out_grad.shape[0]
    wide = GROUP * HEAD_DIM
    bf16 = jnp.bfloat16
    slot = (peers, BLOCK_ROWS, HEAD_DIM)
    part = (peers // parts, BLOCK_ROWS)
    return pl.pallas_call(
        functools.partial(attention_kernel, len(done)),
        grid_spec=pltpu.PrefetchScalarGridSpec(
            num_scalar_prefetch=2,
            grid=(count,),
            in_specs=[
                pl.BlockSpec((peers, BLOCK_ROWS, wide), lambda g, *_: (0, 0, g)),
                pl.BlockSpec(slot, lambda g, *_: (0, 0, key_at + first + g)),
                pl.BlockSpec((rows, HEAD_DIM), lambda g, *_: (0, first + g)),
                pl.BlockSpec((rows, wide), lambda g, *_: (0, first + g)),
                pl.BlockSpec((1, rows), lambda g, *_: (0, 0)),
                pl.BlockSpec((rows, 1), lambda g, *_: (0, 0)),
            ]
            + [pl.BlockSpec(memory_space=pl.ANY)] * len(done),
            out_specs=[
                pl.BlockSpec((rows, wide), lambda g, *_: (0, first + g)),
                pl.BlockSpec((rows, HEAD_DIM), lambda g, *_: (0, first + g)),
                pl.BlockSpec((rows, HEAD_DIM), lambda g, *_: (0, first + g)),
            ]
            + [pl.BlockSpec(part + (HEAD_DIM,), lambda g, *_: (0, 0, g))] * parts,
            scratch_shapes=[
                pltpu.VMEM((rows, wide), bf16),
                pltpu.VMEM((rows, HEAD_DIM), bf16),
                pltpu.VMEM((rows, rows), jnp.float32),
                pltpu.VMEM((rows, HEAD_DIM), jnp.float32),
                pltpu.VMEM((rows, HEAD_DIM), jnp.float32),
            ],
        ),
        out_shape=[
            jax.ShapeDtypeStruct((rows, KV_HEADS * wide), bf16),
            jax.ShapeDtypeStruct((rows, KV_HEADS * HEAD_DIM), bf16),
            jax.ShapeDtypeStruct((rows, KV_HEADS * HEAD_DIM), bf16),
        ]
        + [jax.ShapeDtypeStruct(part + (count * HEAD_DIM,), bf16)] * parts,
        input_output_aliases={8 + i: i for i in range(len(done))},
        cost_estimate=pl.CostEstimate(
            flops=12 * rows * rows * HEAD_DIM * GROUP * count,
            bytes_accessed=10 * rows * wide * count,
            transcendentals=rows * rows * GROUP * count,
        ),
        name="attention_backward",
    )(
        take, back, arrived_q, arrived_k, packed_v, out_grad, doc_ids, doc_ids.reshape(rows, 1),
        *done,
    )


def weight_kernel(table, core, turned_ref, *refs):
    *landed, out_ref, home = refs
    rows = home.shape[0] // 2

    @pl.when(pl.program_id(0) == 0)
    def _():
        if len(landed) == 2:
            for half in range(2):
                for b in range(rows // BLOCK_ROWS):
                    place = slice(half * rows + b * BLOCK_ROWS, half * rows + (b + 1) * BLOCK_ROWS)
                    home[place, :] = landed[half][table[half, b]]
        else:
            for half in range(2):
                slot = core[0] if half == 0 else 1 - core[0]
                for o, ref in enumerate(landed):

                    @pl.when(table[half, o] >= 0)
                    def _():
                        at = half * rows + table[half, o] * BLOCK_ROWS
                        home[pl.ds(pl.multiple_of(at, 16), BLOCK_ROWS), :] = ref[slot]

    part = jnp.dot(turned_ref[...], home[...], preferred_element_type=jnp.float32)
    columns, share, inner, width = out_ref.shape
    part = part.reshape(share, columns, inner, width).astype(out_ref.dtype)
    for i in range(share):
        out_ref[:, i] = part[i]


def weight_part(table, core, turned, landed, columns, steps):
    depth, rows = turned.shape
    width = landed[0].shape[2]
    inner = depth // steps // columns
    share = 4
    tile = share * inner * columns
    return pl.pallas_call(
        weight_kernel,
        grid_spec=pltpu.PrefetchScalarGridSpec(
            num_scalar_prefetch=2,
            grid=(steps // share,),
            in_specs=[pl.BlockSpec((tile, rows), lambda z, *_: (z, 0))]
            + [pl.BlockSpec(array.shape, lambda z, *_: (0, 0, 0)) for array in landed],
            out_specs=pl.BlockSpec(
                (columns, share, inner, width), lambda z, *_: (0, z, 0, 0)
            ),
            scratch_shapes=[pltpu.VMEM((rows, width), jnp.bfloat16)],
        ),
        out_shape=jax.ShapeDtypeStruct((columns, steps, inner, width), jnp.bfloat16),
        name="weight_part",
    )(table, core, turned, *landed)


def ring(count, step, stride=1):
    size = count[1]
    return [
        (i, i + ((i // stride % size + step) % size - i // stride % size) * stride)
        for i in range(count[0])
    ]


def far_first(count):
    return sorted(range(count), key=lambda d: -min(d, count - d))


def gather_ring(array, at, size, shift, relay):
    cut = array.shape[0] // 2
    before, after = shift(array, 1), shift(array, -1)
    if relay:
        far = [(0, shift(before[:cut], 1)), (cut, shift(after[cut:], -1))]
    else:
        far = [(0, shift(array, 2))]
    pieces = [(0, 0, array), (1, 0, before), (3, 0, after)] + [(2, row, part) for row, part in far]
    out = jnp.zeros((size,) + array.shape, array.dtype)
    none = (0,) * (array.ndim - 1)
    for step, row, piece in pieces:
        out = lax.dynamic_update_slice(out, piece[None], ((at + size - step) % size, row) + none)
    return out


def local(normed, queries, key_rows, out_grad, value_weight, doc_ids, send_to, take_from):
    dp_count = lax.axis_size("dp")
    fsdp_count = lax.axis_size("fsdp")
    planes = dp_count // 2
    side = int(fsdp_count**0.5)
    rows, depth = normed.shape
    blocks = rows // BLOCK_ROWS
    grad_scale = (rows * dp_count * fsdp_count) ** (-0.5)
    send, take = send_to[0], take_from[0]
    dp, fsdp = lax.axis_index("dp"), lax.axis_index("fsdp")
    core, plane_at = dp % 2, dp // 2
    core_of = core.reshape(1)
    cores = [(i, i ^ 1) for i in range(dp_count)]
    hops = far_first(planes)
    number = jnp.arange(blocks, dtype=jnp.int32)
    hop_steps = jnp.array(hops, jnp.int32)
    pair = jnp.arange(2, dtype=jnp.int32)

    def along_z(arrays):
        return [
            a if d == 0 else lax.ppermute(a, "dp", ring((dp_count, planes), d, 2))
            for a, d in zip(arrays, hops)
        ]

    def swap(arrays):
        return [lax.ppermute(a, "dp", cores) for a in arrays]

    def along_x(array, step):
        return lax.ppermute(array, "fsdp", ring((fsdp_count, side), step, side))

    def along_y(array, step):
        return lax.ppermute(array, "fsdp", ring((fsdp_count, side), step, 1))

    def which(table, devices):
        return jnp.sum(jnp.where(table[None, :] == devices[:, None], number + 1, 0), axis=1) - 1

    wide = queries.shape[1] // 2
    keys = key_rows.shape[1]
    slots = outgoing_slots(send, [(queries, wide, 0), (key_rows, keys, 0)], dp_count)
    arrived_one = lax.all_to_all(slots, "dp", 0, 0, tiled=True)
    slots = outgoing_slots(send, [(queries, wide, 1)], dp_count)
    arrived_two = lax.all_to_all(slots, "dp", 0, 0, tiled=True)

    width = value_weight.shape[1] // 2
    half = lax.dynamic_slice_in_dim(value_weight, core * width, width, axis=1)
    x, y = fsdp // side, fsdp % side
    line = gather_ring(half, x, side, along_x, False)
    own = gather_ring(line, y, side, along_y, True)
    own = jnp.transpose(own, (1, 0, 2, 3)).reshape(depth, width)
    (other,) = swap([own])

    onward = (((plane_at + hop_steps) % planes * 2)[:, None] + pair).reshape(-1)
    origin = (plane_at + planes - hop_steps) % planes * 2
    origin = jnp.concatenate([origin + core, origin + 1 - core])
    block = jnp.maximum(which(send, onward), 0)
    back = jnp.maximum(which(take, onward), 0)
    place = which(take, origin)
    leaving = value_blocks(core_of, block, normed, own, other)
    landed = along_z(leaving)
    leave = [lax.dynamic_index_in_dim(a, 1 - core, 0, keepdims=False) for a in landed]
    (swapped,) = swap([jnp.stack(leave)])
    packed_v = pack(core_of, place, landed, swapped, rows)

    column = 2 * jnp.arange(planes, dtype=jnp.int32)
    tile = depth // dp_count
    picked = pick_columns(column + 1 - core, normed, tile)
    (got,) = swap([picked])
    turned = turn_columns(column + core, normed, got, tile)
    (partner,) = swap([send_to])
    sends = jnp.concatenate([send_to, partner], axis=0)
    homes = jnp.stack([which(send, origin), which(partner[0], origin)])

    half_groups = KV_HEADS // 2
    key_at = wide // HEAD_DIM
    done = attention(
        take, back, arrived_one, arrived_one, packed_v, out_grad, doc_ids,
        0, half_groups, key_at, (), planes,
    )
    done, returning_one = done[:3], done[3:]
    landed_one = along_z(returning_one)
    landed_one += swap(landed_one)
    query_grad, key_grad, value_grad, returning = attention(
        take, back, arrived_two, arrived_one, packed_v, out_grad, doc_ids,
        half_groups, half_groups, key_at, done, 1,
    )
    landed_two = lax.all_to_all(returning, "dp", 0, 0, tiled=True)
    chip_one = weight_part(homes, core_of, turned, landed_one, fsdp_count, planes)
    chips_one = lax.all_to_all(chip_one, "fsdp", 0, 0, tiled=True)
    landed_two = [landed_two] + swap([landed_two])
    chip_two = weight_part(sends, core_of, turned, landed_two, fsdp_count, planes)
    input_grad = input_gradient(core_of, value_grad, own, other)
    chips_two = lax.all_to_all(chip_two, "fsdp", 0, 0, tiled=True)

    plane = jnp.concatenate(
        [jnp.sum(a.astype(jnp.float32), axis=0) for a in (chips_one, chips_two)], axis=-1
    ).astype(jnp.bfloat16)
    groups = [list(range(c, dp_count, 2)) for c in range(2)]
    parts = lax.all_to_all(plane, "dp", 0, 0, axis_index_groups=groups, tiled=True)
    weight_grad = jnp.sum(parts.astype(jnp.float32), axis=0) * grad_scale
    return (query_grad, key_grad, input_grad, weight_grad)


def solution(mesh):
    rows = P(("dp", "fsdp"), None)
    return jax.shard_map(
        local,
        mesh=mesh,
        in_specs=(rows, rows, rows, rows, P("fsdp", None), rows, rows, rows),
        out_specs=(rows, rows, rows, rows),
        check_vma=False,
    )
```

```python
import functools

import jax
import jax.numpy as jnp
from jax import lax
from jax.experimental import pallas as pl
from jax.experimental.pallas import tpu as pltpu
from jax.sharding import PartitionSpec as P


HEADS = 16
KV_HEADS = 4
HEAD_DIM = 128
GROUP = HEADS // KV_HEADS
BLOCK_ROWS = 48
QUERY_TILE = 128
EARLY = 3


def outgoing_kernel(columns, send, *refs):
    count = len(columns)
    sources, out, held = refs[:count], refs[count], refs[count + 1 : -2]
    came, gone = refs[-2:]
    blocks = held[0].shape[0]

    def fetch(b, i):
        width, first = columns[i]
        rows = pl.ds(b * BLOCK_ROWS, BLOCK_ROWS)
        part = sources[i].at[rows, pl.ds(first * width, width)]
        return pltpu.make_async_copy(part, held[i].at[b], came.at[b, i])

    def store(b, i):
        at = sum(width for width, _ in columns[:i])
        part = out.at[send[b], :, pl.ds(at, columns[i][0])]
        return pltpu.make_async_copy(held[i].at[b], part, gone.at[b, i])

    steps = [(b, i) for b in range(blocks) for i in range(count)]
    for b, i in steps:
        fetch(b, i).start()
    for b, i in steps:
        fetch(b, i).wait()
        store(b, i).start()
    for b, i in steps:
        store(b, i).wait()


def outgoing_slots(send, sources, peers):
    blocks = send.shape[0]
    columns = tuple((width, first) for _, width, first in sources)
    width = sum(part for part, _ in columns)
    dtype = sources[0][0].dtype
    anywhere = pl.BlockSpec(memory_space=pl.ANY)
    return pl.pallas_call(
        functools.partial(outgoing_kernel, columns),
        grid_spec=pltpu.PrefetchScalarGridSpec(
            num_scalar_prefetch=1,
            grid=(1,),
            in_specs=[anywhere] * len(columns),
            out_specs=anywhere,
            scratch_shapes=[pltpu.VMEM((blocks, BLOCK_ROWS, part), dtype) for part, _ in columns]
            + [pltpu.SemaphoreType.DMA((blocks, len(columns)))] * 2,
        ),
        out_shape=jax.ShapeDtypeStruct((peers, BLOCK_ROWS, width), dtype),
        name="outgoing_slots",
    )(send, *(array for array, _, _ in sources))


def halves(core, ref, width):
    own = ref.at[:, pl.ds(pl.multiple_of(core * width, width), width)]
    other = ref.at[:, pl.ds(pl.multiple_of((1 - core) * width, width), width)]
    return own, other


def values_kernel(core, block, normed_ref, own_ref, other_ref, *rest):
    outs, total = rest[:-1], rest[-1]
    step = pl.program_id(0)
    own, other = halves(core[0], total, own_ref.shape[1])

    @pl.when(step == 0)
    def _():
        total[...] = jnp.zeros_like(total)

    rows = normed_ref[...]
    own[...] += jnp.dot(rows, own_ref[...], preferred_element_type=jnp.float32)
    other[...] += jnp.dot(rows, other_ref[...], preferred_element_type=jnp.float32)

    @pl.when(step == pl.num_programs(0) - 1)
    def _():
        for o, out in enumerate(outs):
            for c in range(out.shape[0]):
                first = pl.multiple_of(block[2 * o + c] * BLOCK_ROWS, 16)
                out[c] = total[pl.ds(first, BLOCK_ROWS), :].astype(out.dtype)


def value_blocks(core, block, normed, own, other):
    rows, depth = normed.shape
    width = own.shape[1]
    slots = block.shape[0] // 2
    tile = depth // 4
    shape = (2, BLOCK_ROWS, 2 * width)
    return pl.pallas_call(
        values_kernel,
        grid_spec=pltpu.PrefetchScalarGridSpec(
            num_scalar_prefetch=2,
            grid=(depth // tile,),
            in_specs=[
                pl.BlockSpec((rows, tile), lambda k, *_: (0, k)),
                pl.BlockSpec((tile, width), lambda k, *_: (k, 0)),
                pl.BlockSpec((tile, width), lambda k, *_: (k, 0)),
            ],
            out_specs=[pl.BlockSpec(shape, lambda k, *_: (0, 0, 0))] * slots,
            scratch_shapes=[pltpu.VMEM((rows, 2 * width), jnp.float32)],
        ),
        out_shape=[jax.ShapeDtypeStruct(shape, normed.dtype)] * slots,
        cost_estimate=pl.CostEstimate(
            flops=4 * rows * width * depth,
            bytes_accessed=2 * (normed.size + own.size + other.size),
            transcendentals=0,
        ),
        name="value_blocks",
    )(core, block, normed, own, other)


def pack_kernel(core, place, *refs):
    out = refs[-1]
    *own, swapped = refs[:-1]
    sources = [ref.at[core[0]] for ref in own] + [swapped.at[o] for o in range(swapped.shape[0])]
    for o, ref in enumerate(sources):

        @pl.when(place[o] >= 0)
        def _():
            first = pl.multiple_of(place[o] * BLOCK_ROWS, 16)
            out[pl.ds(first, BLOCK_ROWS), :] = ref[...]


def pack(core, place, own, swapped, rows):
    width = swapped.shape[2]
    shape = (2, BLOCK_ROWS, width)
    return pl.pallas_call(
        pack_kernel,
        grid_spec=pltpu.PrefetchScalarGridSpec(
            num_scalar_prefetch=2,
            grid=(1,),
            in_specs=[pl.BlockSpec(shape, lambda k, *_: (0, 0, 0))] * len(own)
            + [pl.BlockSpec(swapped.shape, lambda k, *_: (0, 0, 0))],
            out_specs=pl.BlockSpec((rows, width), lambda k, *_: (0, 0)),
        ),
        out_shape=jax.ShapeDtypeStruct((rows, width), swapped.dtype),
        name="pack_values",
    )(core, place, *own, swapped)


def pick_kernel(tile, column, source, out, held, came, gone):
    steps = held.shape[0]

    def fetch(z):
        first = pl.multiple_of(column[z] * tile, tile)
        return pltpu.make_async_copy(source.at[:, pl.ds(first, tile)], held.at[z], came.at[z])

    def store(z):
        return pltpu.make_async_copy(held.at[z], out.at[:, pl.ds(z * tile, tile)], gone.at[z])

    for z in range(steps):
        fetch(z).start()
    for z in range(steps):
        fetch(z).wait()
        store(z).start()
    for z in range(steps):
        store(z).wait()


def pick_columns(column, array, tile):
    rows = array.shape[0]
    steps = column.shape[0]
    anywhere = pl.BlockSpec(memory_space=pl.ANY)
    return pl.pallas_call(
        functools.partial(pick_kernel, tile),
        grid_spec=pltpu.PrefetchScalarGridSpec(
            num_scalar_prefetch=1,
            grid=(1,),
            in_specs=[anywhere],
            out_specs=anywhere,
            scratch_shapes=[
                pltpu.VMEM((steps, rows, tile), array.dtype),
                pltpu.SemaphoreType.DMA((steps,)),
                pltpu.SemaphoreType.DMA((steps,)),
            ],
        ),
        out_shape=jax.ShapeDtypeStruct((rows, tile * steps), array.dtype),
        name="pick_columns",
    )(column, array)


def turn_kernel(column, own_ref, got_ref, out_ref):
    rows = own_ref.shape[0]
    out_ref[:, :rows] = own_ref[...].T
    out_ref[:, rows:] = got_ref[...].T


def turn_columns(column, array, got, tile):
    rows = array.shape[0]
    steps = column.shape[0]
    return pl.pallas_call(
        turn_kernel,
        grid_spec=pltpu.PrefetchScalarGridSpec(
            num_scalar_prefetch=1,
            grid=(steps,),
            in_specs=[
                pl.BlockSpec((rows, tile), lambda z, column: (0, column[z])),
                pl.BlockSpec((rows, tile), lambda z, column: (0, z)),
            ],
            out_specs=pl.BlockSpec((tile, 2 * rows), lambda z, column: (z, 0)),
        ),
        out_shape=jax.ShapeDtypeStruct((tile * steps, 2 * rows), array.dtype),
        name="turn_columns",
    )(column, array, got)


def input_grad_kernel(core, grad_ref, own_ref, other_ref, out_ref):
    own, other = halves(core[0], grad_ref, own_ref.shape[1])
    nt = (((1,), (1,)), ((), ()))
    total = lax.dot_general(own[...], own_ref[...], nt, preferred_element_type=jnp.float32)
    total += lax.dot_general(other[...], other_ref[...], nt, preferred_element_type=jnp.float32)
    out_ref[...] = total.astype(out_ref.dtype)


def input_gradient(core, value_grad, own, other):
    rows = value_grad.shape[0]
    depth, width = own.shape
    tile = depth // 8
    return pl.pallas_call(
        input_grad_kernel,
        grid_spec=pltpu.PrefetchScalarGridSpec(
            num_scalar_prefetch=1,
            grid=(depth // tile,),
            in_specs=[
                pl.BlockSpec((rows, 2 * width), lambda k, *_: (0, 0)),
                pl.BlockSpec((tile, width), lambda k, *_: (k, 0)),
                pl.BlockSpec((tile, width), lambda k, *_: (k, 0)),
            ],
            out_specs=pl.BlockSpec((rows, tile), lambda k, *_: (0, k)),
        ),
        out_shape=jax.ShapeDtypeStruct((rows, depth), value_grad.dtype),
        cost_estimate=pl.CostEstimate(
            flops=4 * rows * width * depth,
            bytes_accessed=2 * (rows * depth + own.size + other.size),
            transcendentals=0,
        ),
        name="input_gradient",
    )(core, value_grad, own, other)


def attention_kernel(take, q_ref, k_ref, v_ref, grad_ref, doc_row, doc_col, *rest):
    query_grad, key_grad, value_grad, returning = rest[-9:-5]
    q_rows, k_rows, bias, key_total, value_total = rest[-5:]
    rows = grad_ref.shape[0]
    blocks = rows // BLOCK_ROWS
    scale = HEAD_DIM ** (-0.5)

    @pl.when(pl.program_id(0) == 0)
    def _():
        i = lax.broadcasted_iota(jnp.int32, (rows, rows), 0)
        j = lax.broadcasted_iota(jnp.int32, (rows, rows), 1)
        allowed = (doc_col[...] == doc_row[...]) & (j <= i)
        bias[...] = jnp.where(allowed, 0.0, -jnp.inf)

    for p in range(blocks):
        place = slice(p * BLOCK_ROWS, (p + 1) * BLOCK_ROWS)
        q_rows[place, :] = q_ref[take[p]]
        k_rows[place, :] = k_ref[take[p]]

    key_total[...] = jnp.zeros_like(key_total)
    value_total[...] = jnp.zeros_like(value_total)
    for start in range(0, rows, QUERY_TILE):
        place = slice(start, start + QUERY_TILE)
        reach = start + QUERY_TILE
        q = jnp.concatenate(
            [q_rows[place, x * HEAD_DIM : (x + 1) * HEAD_DIM] for x in range(GROUP)], axis=0
        )
        g = jnp.concatenate(
            [grad_ref[place, x * HEAD_DIM : (x + 1) * HEAD_DIM] for x in range(GROUP)], axis=0
        )
        k = k_rows[:reach, :]
        v = v_ref[:reach, :]
        nt = (((1,), (1,)), ((), ()))
        tn = (((0,), (0,)), ((), ()))
        scores = lax.dot_general(q, k, nt, preferred_element_type=jnp.float32) * scale
        hide = bias[place, :reach]
        scores = scores + jnp.concatenate([hide] * GROUP, axis=0)
        peak = jnp.max(scores, axis=-1, keepdims=True)
        exponent = jnp.exp(scores - peak)
        probs = exponent / jnp.sum(exponent, axis=-1, keepdims=True)
        half = probs.astype(jnp.bfloat16)
        attn = jnp.dot(half, v, preferred_element_type=jnp.float32)
        delta = jnp.sum(g.astype(jnp.float32) * attn, axis=-1, keepdims=True)
        prob_grad = lax.dot_general(g, v, nt, preferred_element_type=jnp.float32)
        score_grad = (probs * (prob_grad - delta) * scale).astype(jnp.bfloat16)
        back = jnp.dot(score_grad, k, preferred_element_type=jnp.float32)
        for x in range(GROUP):
            query_grad[place, x * HEAD_DIM : (x + 1) * HEAD_DIM] = back[
                x * QUERY_TILE : (x + 1) * QUERY_TILE
            ].astype(query_grad.dtype)
        key_total[:reach, :] += lax.dot_general(
            score_grad, q, tn, preferred_element_type=jnp.float32
        )
        value_total[:reach, :] += lax.dot_general(half, g, tn, preferred_element_type=jnp.float32)
    key_grad[...] = key_total[...].astype(key_grad.dtype)
    value_grad[...] = value_total[...].astype(value_grad.dtype)
    returning[...] = jnp.zeros_like(returning)
    for p in range(blocks):
        place = slice(p * BLOCK_ROWS, (p + 1) * BLOCK_ROWS)
        returning[take[p]] = value_total[place, :].astype(returning.dtype)


def attention(take, arrived_q, arrived_k, packed_v, out_grad, doc_ids, first, count, key_at, done):
    peers = arrived_q.shape[0]
    rows = out_grad.shape[0]
    wide = GROUP * HEAD_DIM
    bf16 = jnp.bfloat16
    slot = (peers, BLOCK_ROWS, HEAD_DIM)
    return pl.pallas_call(
        attention_kernel,
        grid_spec=pltpu.PrefetchScalarGridSpec(
            num_scalar_prefetch=1,
            grid=(count,),
            in_specs=[
                pl.BlockSpec((peers, BLOCK_ROWS, wide), lambda g, take: (0, 0, g)),
                pl.BlockSpec(slot, lambda g, take: (0, 0, key_at + first + g)),
                pl.BlockSpec((rows, HEAD_DIM), lambda g, take: (0, first + g)),
                pl.BlockSpec((rows, wide), lambda g, take: (0, first + g)),
                pl.BlockSpec((1, rows), lambda g, take: (0, 0)),
                pl.BlockSpec((rows, 1), lambda g, take: (0, 0)),
            ]
            + [pl.BlockSpec(memory_space=pl.ANY)] * len(done),
            out_specs=[
                pl.BlockSpec((rows, wide), lambda g, take: (0, first + g)),
                pl.BlockSpec((rows, HEAD_DIM), lambda g, take: (0, first + g)),
                pl.BlockSpec((rows, HEAD_DIM), lambda g, take: (0, first + g)),
                pl.BlockSpec(slot, lambda g, take: (0, 0, first + g)),
            ],
            scratch_shapes=[
                pltpu.VMEM((rows, wide), bf16),
                pltpu.VMEM((rows, HEAD_DIM), bf16),
                pltpu.VMEM((rows, rows), jnp.float32),
                pltpu.VMEM((rows, HEAD_DIM), jnp.float32),
                pltpu.VMEM((rows, HEAD_DIM), jnp.float32),
            ],
        ),
        out_shape=[
            jax.ShapeDtypeStruct((rows, KV_HEADS * wide), bf16),
            jax.ShapeDtypeStruct((rows, KV_HEADS * HEAD_DIM), bf16),
            jax.ShapeDtypeStruct((rows, KV_HEADS * HEAD_DIM), bf16),
            jax.ShapeDtypeStruct((peers, BLOCK_ROWS, KV_HEADS * HEAD_DIM), bf16),
        ],
        input_output_aliases={7 + i: i for i in range(len(done))},
        cost_estimate=pl.CostEstimate(
            flops=12 * rows * rows * HEAD_DIM * GROUP * count,
            bytes_accessed=10 * rows * wide * count,
            transcendentals=rows * rows * GROUP * count,
        ),
        name="attention_backward",
    )(take, arrived_q, arrived_k, packed_v, out_grad, doc_ids, doc_ids.reshape(rows, 1), *done)


def weight_kernel(send, turned_ref, landed_ref, swapped_ref, out_ref, home):
    rows = home.shape[0] // 2

    @pl.when(pl.program_id(0) == 0)
    def _():
        for b in range(rows // BLOCK_ROWS):
            place = slice(b * BLOCK_ROWS, (b + 1) * BLOCK_ROWS)
            home[place, :] = landed_ref[send[0, b]]
        for b in range(rows // BLOCK_ROWS):
            place = slice(rows + b * BLOCK_ROWS, rows + (b + 1) * BLOCK_ROWS)
            home[place, :] = swapped_ref[send[1, b]]

    part = jnp.dot(turned_ref[...], home[...], preferred_element_type=jnp.float32)
    columns, share, inner, width = out_ref.shape
    part = part.reshape(share, columns, inner, width).astype(out_ref.dtype)
    for i in range(share):
        out_ref[:, i] = part[i]


def weight_part(send, turned, landed, swapped, columns, steps):
    depth, rows = turned.shape
    peers, _, width = landed.shape
    inner = depth // steps // columns
    share = 4
    tile = share * inner * columns
    return pl.pallas_call(
        weight_kernel,
        grid_spec=pltpu.PrefetchScalarGridSpec(
            num_scalar_prefetch=1,
            grid=(steps // share,),
            in_specs=[
                pl.BlockSpec((tile, rows), lambda z, send: (z, 0)),
                pl.BlockSpec((peers, BLOCK_ROWS, width), lambda z, send: (0, 0, 0)),
                pl.BlockSpec((peers, BLOCK_ROWS, width), lambda z, send: (0, 0, 0)),
            ],
            out_specs=pl.BlockSpec((columns, share, inner, width), lambda z, send: (0, z, 0, 0)),
            scratch_shapes=[pltpu.VMEM((rows, width), jnp.bfloat16)],
        ),
        out_shape=jax.ShapeDtypeStruct((columns, steps, inner, width), jnp.bfloat16),
        name="weight_part",
    )(send, turned, landed, swapped)


def ring(count, step, stride=1):
    size = count[1]
    return [
        (i, i + ((i // stride % size + step) % size - i // stride % size) * stride)
        for i in range(count[0])
    ]


def far_first(count):
    return sorted(range(count), key=lambda d: -min(d, count - d))


def gather_ring(array, at, size, shift, relay):
    cut = array.shape[0] // 2
    before, after = shift(array, 1), shift(array, -1)
    if relay:
        far = [(0, shift(before[:cut], 1)), (cut, shift(after[cut:], -1))]
    else:
        far = [(0, shift(array, 2))]
    pieces = [(0, 0, array), (1, 0, before), (3, 0, after)] + [(2, row, part) for row, part in far]
    out = jnp.zeros((size,) + array.shape, array.dtype)
    none = (0,) * (array.ndim - 1)
    for step, row, piece in pieces:
        out = lax.dynamic_update_slice(out, piece[None], ((at + size - step) % size, row) + none)
    return out


def local(normed, queries, key_rows, out_grad, value_weight, doc_ids, send_to, take_from):
    dp_count = lax.axis_size("dp")
    fsdp_count = lax.axis_size("fsdp")
    planes = dp_count // 2
    side = int(fsdp_count**0.5)
    rows, depth = normed.shape
    blocks = rows // BLOCK_ROWS
    grad_scale = (rows * dp_count * fsdp_count) ** (-0.5)
    send, take = send_to[0], take_from[0]
    dp, fsdp = lax.axis_index("dp"), lax.axis_index("fsdp")
    core, plane_at = dp % 2, dp // 2
    core_of = core.reshape(1)
    cores = [(i, i ^ 1) for i in range(dp_count)]
    hops = far_first(planes)
    number = jnp.arange(blocks, dtype=jnp.int32)
    hop_steps = jnp.array(hops, jnp.int32)
    pair = jnp.arange(2, dtype=jnp.int32)

    def along_z(arrays):
        return [
            a if d == 0 else lax.ppermute(a, "dp", ring((dp_count, planes), d, 2))
            for a, d in zip(arrays, hops)
        ]

    def swap(arrays):
        return [lax.ppermute(a, "dp", cores) for a in arrays]

    def along_x(array, step):
        return lax.ppermute(array, "fsdp", ring((fsdp_count, side), step, side))

    def along_y(array, step):
        return lax.ppermute(array, "fsdp", ring((fsdp_count, side), step, 1))

    def which(table, devices):
        return jnp.sum(jnp.where(table[None, :] == devices[:, None], number + 1, 0), axis=1) - 1

    late = KV_HEADS - EARLY
    wide = GROUP * HEAD_DIM
    keys = key_rows.shape[1]
    slots = outgoing_slots(send, [(queries, EARLY * wide, 0), (key_rows, keys, 0)], dp_count)
    arrived_one = lax.all_to_all(slots, "dp", 0, 0, tiled=True)
    slots = outgoing_slots(send, [(queries, wide, EARLY + g) for g in range(late)], dp_count)
    arrived_two = lax.all_to_all(slots, "dp", 0, 0, tiled=True)

    width = value_weight.shape[1] // 2
    half = lax.dynamic_slice_in_dim(value_weight, core * width, width, axis=1)
    x, y = fsdp // side, fsdp % side
    line = gather_ring(half, x, side, along_x, False)
    own = gather_ring(line, y, side, along_y, True)
    own = jnp.transpose(own, (1, 0, 2, 3)).reshape(depth, width)
    (other,) = swap([own])

    onward = (((plane_at + hop_steps) % planes * 2)[:, None] + pair).reshape(-1)
    origin = (plane_at + planes - hop_steps) % planes * 2
    origin = jnp.concatenate([origin + core, origin + 1 - core])
    block = jnp.maximum(which(send, onward), 0)
    place = which(take, origin)
    leaving = value_blocks(core_of, block, normed, own, other)
    landed = along_z(leaving)
    leave = [lax.dynamic_index_in_dim(a, 1 - core, 0, keepdims=False) for a in landed]
    (swapped,) = swap([jnp.stack(leave)])
    packed_v = pack(core_of, place, landed, swapped, rows)

    column = 2 * jnp.arange(planes, dtype=jnp.int32)
    tile = depth // dp_count
    picked = pick_columns(column + 1 - core, normed, tile)
    (got,) = swap([picked])
    turned = turn_columns(column + core, normed, got, tile)
    (partner,) = swap([send_to])
    sends = jnp.concatenate([send_to, partner], axis=0)

    key_at = EARLY * GROUP
    done = attention(
        take, arrived_one, arrived_one, packed_v, out_grad, doc_ids,
        0, EARLY, key_at, (),
    )
    query_grad, key_grad, value_grad, returning = attention(
        take, arrived_two, arrived_one, packed_v, out_grad, doc_ids,
        EARLY, late, key_at, done,
    )
    landed = lax.all_to_all(returning, "dp", 0, 0, tiled=True)
    (swapped,) = swap([landed])
    input_grad = input_gradient(core_of, value_grad, own, other)

    chip = weight_part(sends, turned, landed, swapped, fsdp_count, planes)
    chips = lax.all_to_all(chip, "fsdp", 0, 0, tiled=True)
    plane = jnp.sum(chips.astype(jnp.float32), axis=0).astype(jnp.bfloat16)
    groups = [list(range(c, dp_count, 2)) for c in range(2)]
    parts = lax.all_to_all(plane, "dp", 0, 0, axis_index_groups=groups, tiled=True)
    weight_grad = jnp.sum(parts.astype(jnp.float32), axis=0) * grad_scale
    return (query_grad, key_grad, input_grad, weight_grad)


def solution(mesh):
    rows = P(("dp", "fsdp"), None)
    return jax.shard_map(
        local,
        mesh=mesh,
        in_specs=(rows, rows, rows, rows, P("fsdp", None), rows, rows, rows),
        out_specs=(rows, rows, rows, rows),
        check_vma=False,
    )
```

```python
import functools

import jax
import jax.numpy as jnp
from jax import lax
from jax.experimental import pallas as pl
from jax.experimental.pallas import tpu as pltpu
from jax.sharding import PartitionSpec as P


HEADS = 16
KV_HEADS = 4
HEAD_DIM = 128
GROUP = HEADS // KV_HEADS
BLOCK_ROWS = 48
QUERY_TILE = 128
EARLY = 3


def outgoing_kernel(columns, send, *refs):
    count = len(columns)
    sources, out, held = refs[:count], refs[count], refs[count + 1 : -2]
    came, gone = refs[-2:]
    blocks = held[0].shape[0]

    def fetch(b, i):
        width, first = columns[i]
        rows = pl.ds(b * BLOCK_ROWS, BLOCK_ROWS)
        part = sources[i].at[rows, pl.ds(first * width, width)]
        return pltpu.make_async_copy(part, held[i].at[b], came.at[b, i])

    def store(b, i):
        at = sum(width for width, _ in columns[:i])
        part = out.at[send[b], :, pl.ds(at, columns[i][0])]
        return pltpu.make_async_copy(held[i].at[b], part, gone.at[b, i])

    steps = [(b, i) for b in range(blocks) for i in range(count)]
    for b, i in steps:
        fetch(b, i).start()
    for b, i in steps:
        fetch(b, i).wait()
        store(b, i).start()
    for b, i in steps:
        store(b, i).wait()


def outgoing_slots(send, sources, peers):
    blocks = send.shape[0]
    columns = tuple((width, first) for _, width, first in sources)
    width = sum(part for part, _ in columns)
    dtype = sources[0][0].dtype
    anywhere = pl.BlockSpec(memory_space=pl.ANY)
    return pl.pallas_call(
        functools.partial(outgoing_kernel, columns),
        grid_spec=pltpu.PrefetchScalarGridSpec(
            num_scalar_prefetch=1,
            grid=(1,),
            in_specs=[anywhere] * len(columns),
            out_specs=anywhere,
            scratch_shapes=[pltpu.VMEM((blocks, BLOCK_ROWS, part), dtype) for part, _ in columns]
            + [pltpu.SemaphoreType.DMA((blocks, len(columns)))] * 2,
        ),
        out_shape=jax.ShapeDtypeStruct((peers, BLOCK_ROWS, width), dtype),
        name="outgoing_slots",
    )(send, *(array for array, _, _ in sources))


def halves(core, ref, width):
    own = ref.at[:, pl.ds(pl.multiple_of(core * width, width), width)]
    other = ref.at[:, pl.ds(pl.multiple_of((1 - core) * width, width), width)]
    return own, other


def values_kernel(core, block, normed_ref, own_ref, other_ref, *rest):
    outs, total = rest[:-1], rest[-1]
    step = pl.program_id(0)
    own, other = halves(core[0], total, own_ref.shape[1])

    @pl.when(step == 0)
    def _():
        total[...] = jnp.zeros_like(total)

    rows = normed_ref[...]
    own[...] += jnp.dot(rows, own_ref[...], preferred_element_type=jnp.float32)
    other[...] += jnp.dot(rows, other_ref[...], preferred_element_type=jnp.float32)

    @pl.when(step == pl.num_programs(0) - 1)
    def _():
        for o, out in enumerate(outs):
            for c in range(out.shape[0]):
                first = pl.multiple_of(block[2 * o + c] * BLOCK_ROWS, 16)
                out[c] = total[pl.ds(first, BLOCK_ROWS), :].astype(out.dtype)


def value_blocks(core, block, normed, own, other):
    rows, depth = normed.shape
    width = own.shape[1]
    slots = block.shape[0] // 2
    tile = depth // 4
    shape = (2, BLOCK_ROWS, 2 * width)
    return pl.pallas_call(
        values_kernel,
        grid_spec=pltpu.PrefetchScalarGridSpec(
            num_scalar_prefetch=2,
            grid=(depth // tile,),
            in_specs=[
                pl.BlockSpec((rows, tile), lambda k, *_: (0, k)),
                pl.BlockSpec((tile, width), lambda k, *_: (k, 0)),
                pl.BlockSpec((tile, width), lambda k, *_: (k, 0)),
            ],
            out_specs=[pl.BlockSpec(shape, lambda k, *_: (0, 0, 0))] * slots,
            scratch_shapes=[pltpu.VMEM((rows, 2 * width), jnp.float32)],
        ),
        out_shape=[jax.ShapeDtypeStruct(shape, normed.dtype)] * slots,
        cost_estimate=pl.CostEstimate(
            flops=4 * rows * width * depth,
            bytes_accessed=2 * (normed.size + own.size + other.size),
            transcendentals=0,
        ),
        name="value_blocks",
    )(core, block, normed, own, other)


def pack_kernel(core, place, *refs):
    out = refs[-1]
    for o, ref in enumerate(refs[:-1]):

        @pl.when(place[o] >= 0)
        def _():
            first = pl.multiple_of(place[o] * BLOCK_ROWS, 16)
            out[pl.ds(first, BLOCK_ROWS), :] = ref[core[0]]


def pack(core, place, blocks, rows):
    width = blocks[0].shape[2]
    shape = (2, BLOCK_ROWS, width)
    return pl.pallas_call(
        pack_kernel,
        grid_spec=pltpu.PrefetchScalarGridSpec(
            num_scalar_prefetch=2,
            grid=(1,),
            in_specs=[pl.BlockSpec(shape, lambda k, *_: (0, 0, 0))] * len(blocks),
            out_specs=pl.BlockSpec((rows, width), lambda k, *_: (0, 0)),
        ),
        out_shape=jax.ShapeDtypeStruct((rows, width), blocks[0].dtype),
        name="pack_values",
    )(core, place, *blocks)


def pick_kernel(tile, column, source, out, held, came, gone):
    steps = held.shape[0]

    def fetch(z):
        first = pl.multiple_of(column[z] * tile, tile)
        return pltpu.make_async_copy(source.at[:, pl.ds(first, tile)], held.at[z], came.at[z])

    def store(z):
        return pltpu.make_async_copy(held.at[z], out.at[:, pl.ds(z * tile, tile)], gone.at[z])

    for z in range(steps):
        fetch(z).start()
    for z in range(steps):
        fetch(z).wait()
        store(z).start()
    for z in range(steps):
        store(z).wait()


def pick_columns(column, array, tile):
    rows = array.shape[0]
    steps = column.shape[0]
    anywhere = pl.BlockSpec(memory_space=pl.ANY)
    return pl.pallas_call(
        functools.partial(pick_kernel, tile),
        grid_spec=pltpu.PrefetchScalarGridSpec(
            num_scalar_prefetch=1,
            grid=(1,),
            in_specs=[anywhere],
            out_specs=anywhere,
            scratch_shapes=[
                pltpu.VMEM((steps, rows, tile), array.dtype),
                pltpu.SemaphoreType.DMA((steps,)),
                pltpu.SemaphoreType.DMA((steps,)),
            ],
        ),
        out_shape=jax.ShapeDtypeStruct((rows, tile * steps), array.dtype),
        name="pick_columns",
    )(column, array)


def turn_kernel(column, own_ref, got_ref, out_ref):
    rows = own_ref.shape[0]
    out_ref[:, :rows] = own_ref[...].T
    out_ref[:, rows:] = got_ref[...].T


def turn_columns(column, array, got, tile):
    rows = array.shape[0]
    steps = column.shape[0]
    return pl.pallas_call(
        turn_kernel,
        grid_spec=pltpu.PrefetchScalarGridSpec(
            num_scalar_prefetch=1,
            grid=(steps,),
            in_specs=[
                pl.BlockSpec((rows, tile), lambda z, column: (0, column[z])),
                pl.BlockSpec((rows, tile), lambda z, column: (0, z)),
            ],
            out_specs=pl.BlockSpec((tile, 2 * rows), lambda z, column: (z, 0)),
        ),
        out_shape=jax.ShapeDtypeStruct((tile * steps, 2 * rows), array.dtype),
        name="turn_columns",
    )(column, array, got)


def input_grad_kernel(core, grad_ref, own_ref, other_ref, out_ref):
    own, other = halves(core[0], grad_ref, own_ref.shape[1])
    nt = (((1,), (1,)), ((), ()))
    total = lax.dot_general(own[...], own_ref[...], nt, preferred_element_type=jnp.float32)
    total += lax.dot_general(other[...], other_ref[...], nt, preferred_element_type=jnp.float32)
    out_ref[...] = total.astype(out_ref.dtype)


def input_gradient(core, value_grad, own, other):
    rows = value_grad.shape[0]
    depth, width = own.shape
    tile = depth // 8
    return pl.pallas_call(
        input_grad_kernel,
        grid_spec=pltpu.PrefetchScalarGridSpec(
            num_scalar_prefetch=1,
            grid=(depth // tile,),
            in_specs=[
                pl.BlockSpec((rows, 2 * width), lambda k, *_: (0, 0)),
                pl.BlockSpec((tile, width), lambda k, *_: (k, 0)),
                pl.BlockSpec((tile, width), lambda k, *_: (k, 0)),
            ],
            out_specs=pl.BlockSpec((rows, tile), lambda k, *_: (0, k)),
        ),
        out_shape=jax.ShapeDtypeStruct((rows, depth), value_grad.dtype),
        cost_estimate=pl.CostEstimate(
            flops=4 * rows * width * depth,
            bytes_accessed=2 * (rows * depth + own.size + other.size),
            transcendentals=0,
        ),
        name="input_gradient",
    )(core, value_grad, own, other)


def attention_kernel(take, q_ref, k_ref, v_ref, grad_ref, doc_row, doc_col, *rest):
    query_grad, key_grad, value_grad, returning = rest[-9:-5]
    q_rows, k_rows, bias, key_total, value_total = rest[-5:]
    rows = grad_ref.shape[0]
    blocks = rows // BLOCK_ROWS
    scale = HEAD_DIM ** (-0.5)

    @pl.when(pl.program_id(0) == 0)
    def _():
        i = lax.broadcasted_iota(jnp.int32, (rows, rows), 0)
        j = lax.broadcasted_iota(jnp.int32, (rows, rows), 1)
        allowed = (doc_col[...] == doc_row[...]) & (j <= i)
        bias[...] = jnp.where(allowed, 0.0, -jnp.inf)

    for p in range(blocks):
        place = slice(p * BLOCK_ROWS, (p + 1) * BLOCK_ROWS)
        q_rows[place, :] = q_ref[take[p]]
        k_rows[place, :] = k_ref[take[p]]

    key_total[...] = jnp.zeros_like(key_total)
    value_total[...] = jnp.zeros_like(value_total)
    for start in range(0, rows, QUERY_TILE):
        place = slice(start, start + QUERY_TILE)
        reach = start + QUERY_TILE
        q = jnp.concatenate(
            [q_rows[place, x * HEAD_DIM : (x + 1) * HEAD_DIM] for x in range(GROUP)], axis=0
        )
        g = jnp.concatenate(
            [grad_ref[place, x * HEAD_DIM : (x + 1) * HEAD_DIM] for x in range(GROUP)], axis=0
        )
        k = k_rows[:reach, :]
        v = v_ref[:reach, :]
        nt = (((1,), (1,)), ((), ()))
        tn = (((0,), (0,)), ((), ()))
        scores = lax.dot_general(q, k, nt, preferred_element_type=jnp.float32) * scale
        hide = bias[place, :reach]
        scores = scores + jnp.concatenate([hide] * GROUP, axis=0)
        peak = jnp.max(scores, axis=-1, keepdims=True)
        exponent = jnp.exp(scores - peak)
        probs = exponent / jnp.sum(exponent, axis=-1, keepdims=True)
        half = probs.astype(jnp.bfloat16)
        attn = jnp.dot(half, v, preferred_element_type=jnp.float32)
        delta = jnp.sum(g.astype(jnp.float32) * attn, axis=-1, keepdims=True)
        prob_grad = lax.dot_general(g, v, nt, preferred_element_type=jnp.float32)
        score_grad = (probs * (prob_grad - delta) * scale).astype(jnp.bfloat16)
        back = jnp.dot(score_grad, k, preferred_element_type=jnp.float32)
        for x in range(GROUP):
            query_grad[place, x * HEAD_DIM : (x + 1) * HEAD_DIM] = back[
                x * QUERY_TILE : (x + 1) * QUERY_TILE
            ].astype(query_grad.dtype)
        key_total[:reach, :] += lax.dot_general(
            score_grad, q, tn, preferred_element_type=jnp.float32
        )
        value_total[:reach, :] += lax.dot_general(half, g, tn, preferred_element_type=jnp.float32)
    key_grad[...] = key_total[...].astype(key_grad.dtype)
    value_grad[...] = value_total[...].astype(value_grad.dtype)
    returning[...] = jnp.zeros_like(returning)
    for p in range(blocks):
        place = slice(p * BLOCK_ROWS, (p + 1) * BLOCK_ROWS)
        returning[take[p]] = value_total[place, :].astype(returning.dtype)


def attention(take, arrived_q, arrived_k, packed_v, out_grad, docs, first, count, key_at, done):
    peers = arrived_q.shape[0]
    rows = out_grad.shape[0]
    wide = GROUP * HEAD_DIM
    bf16 = jnp.bfloat16
    slot = (peers, BLOCK_ROWS, HEAD_DIM)
    return pl.pallas_call(
        attention_kernel,
        grid_spec=pltpu.PrefetchScalarGridSpec(
            num_scalar_prefetch=1,
            grid=(count,),
            in_specs=[
                pl.BlockSpec((peers, BLOCK_ROWS, wide), lambda g, take: (0, 0, g)),
                pl.BlockSpec(slot, lambda g, take: (0, 0, key_at + first + g)),
                pl.BlockSpec((rows, HEAD_DIM), lambda g, take: (0, first + g)),
                pl.BlockSpec((rows, wide), lambda g, take: (0, first + g)),
                pl.BlockSpec((1, rows), lambda g, take: (0, 0)),
                pl.BlockSpec((rows, 1), lambda g, take: (0, 0)),
            ]
            + [pl.BlockSpec(memory_space=pl.ANY)] * len(done),
            out_specs=[
                pl.BlockSpec((rows, wide), lambda g, take: (0, first + g)),
                pl.BlockSpec((rows, HEAD_DIM), lambda g, take: (0, first + g)),
                pl.BlockSpec((rows, HEAD_DIM), lambda g, take: (0, first + g)),
                pl.BlockSpec(slot, lambda g, take: (0, 0, first + g)),
            ],
            scratch_shapes=[
                pltpu.VMEM((rows, wide), bf16),
                pltpu.VMEM((rows, HEAD_DIM), bf16),
                pltpu.VMEM((rows, rows), jnp.float32),
                pltpu.VMEM((rows, HEAD_DIM), jnp.float32),
                pltpu.VMEM((rows, HEAD_DIM), jnp.float32),
            ],
        ),
        out_shape=[
            jax.ShapeDtypeStruct((rows, KV_HEADS * wide), bf16),
            jax.ShapeDtypeStruct((rows, KV_HEADS * HEAD_DIM), bf16),
            jax.ShapeDtypeStruct((rows, KV_HEADS * HEAD_DIM), bf16),
            jax.ShapeDtypeStruct((peers, BLOCK_ROWS, KV_HEADS * HEAD_DIM), bf16),
        ],
        input_output_aliases={7 + i: i for i in range(len(done))},
        cost_estimate=pl.CostEstimate(
            flops=12 * rows * rows * HEAD_DIM * GROUP * count,
            bytes_accessed=10 * rows * wide * count,
            transcendentals=rows * rows * GROUP * count,
        ),
        name="attention_backward",
    )(take, arrived_q, arrived_k, packed_v, out_grad, *docs, *done)


def weight_kernel(send, turned_ref, landed_ref, swapped_ref, out_ref, home):
    rows = home.shape[0] // 2

    @pl.when(pl.program_id(0) == 0)
    def _():
        for b in range(rows // BLOCK_ROWS):
            place = slice(b * BLOCK_ROWS, (b + 1) * BLOCK_ROWS)
            home[place, :] = landed_ref[send[0, b]]
        for b in range(rows // BLOCK_ROWS):
            place = slice(rows + b * BLOCK_ROWS, rows + (b + 1) * BLOCK_ROWS)
            home[place, :] = swapped_ref[send[1, b]]

    part = jnp.dot(turned_ref[...], home[...], preferred_element_type=jnp.float32)
    columns, share, inner, width = out_ref.shape
    part = part.reshape(share, columns, inner, width).astype(out_ref.dtype)
    for i in range(share):
        out_ref[:, i] = part[i]


def weight_part(send, turned, landed, swapped, columns, steps):
    depth, rows = turned.shape
    peers, _, width = landed.shape
    inner = depth // steps // columns
    share = 4
    tile = share * inner * columns
    return pl.pallas_call(
        weight_kernel,
        grid_spec=pltpu.PrefetchScalarGridSpec(
            num_scalar_prefetch=1,
            grid=(steps // share,),
            in_specs=[
                pl.BlockSpec((tile, rows), lambda z, send: (z, 0)),
                pl.BlockSpec((peers, BLOCK_ROWS, width), lambda z, send: (0, 0, 0)),
                pl.BlockSpec((peers, BLOCK_ROWS, width), lambda z, send: (0, 0, 0)),
            ],
            out_specs=pl.BlockSpec((columns, share, inner, width), lambda z, send: (0, z, 0, 0)),
            scratch_shapes=[pltpu.VMEM((rows, width), jnp.bfloat16)],
        ),
        out_shape=jax.ShapeDtypeStruct((columns, steps, inner, width), jnp.bfloat16),
        name="weight_part",
    )(send, turned, landed, swapped)


def ring(count, step, stride=1):
    size = count[1]
    return [
        (i, i + ((i // stride % size + step) % size - i // stride % size) * stride)
        for i in range(count[0])
    ]


def far_first(count):
    return sorted(range(count), key=lambda d: -min(d, count - d))


def gather_ring(array, at, size, shift, relay):
    cut = array.shape[0] // 2
    before, after = shift(array, 1), shift(array, -1)
    if relay:
        far = [(0, shift(before[:cut], 1)), (cut, shift(after[cut:], -1))]
    else:
        far = [(0, shift(array, 2))]
    pieces = [(0, 0, array), (1, 0, before), (3, 0, after)] + [(2, row, part) for row, part in far]
    out = jnp.zeros((size,) + array.shape, array.dtype)
    none = (0,) * (array.ndim - 1)
    for step, row, piece in pieces:
        out = lax.dynamic_update_slice(out, piece[None], ((at + size - step) % size, row) + none)
    return out


def local(normed, queries, key_rows, out_grad, value_weight, doc_ids, send_to, take_from):
    dp_count = lax.axis_size("dp")
    fsdp_count = lax.axis_size("fsdp")
    planes = dp_count // 2
    side = int(fsdp_count**0.5)
    rows, depth = normed.shape
    blocks = rows // BLOCK_ROWS
    grad_scale = (rows * dp_count * fsdp_count) ** (-0.5)
    send, take = send_to[0], take_from[0]
    dp, fsdp = lax.axis_index("dp"), lax.axis_index("fsdp")
    core, plane_at = dp % 2, dp // 2
    core_of = core.reshape(1)
    cores = [(i, i ^ 1) for i in range(dp_count)]
    hops = far_first(planes)
    number = jnp.arange(blocks, dtype=jnp.int32)
    hop_steps = jnp.array(hops, jnp.int32)
    pair = jnp.arange(2, dtype=jnp.int32)

    def along_z(arrays):
        return [
            a if d == 0 else lax.ppermute(a, "dp", ring((dp_count, planes), d, 2))
            for a, d in zip(arrays, hops)
        ]

    def swap(arrays):
        return [lax.ppermute(a, "dp", cores) for a in arrays]

    def along_x(array, step):
        return lax.ppermute(array, "fsdp", ring((fsdp_count, side), step, side))

    def along_y(array, step):
        return lax.ppermute(array, "fsdp", ring((fsdp_count, side), step, 1))

    def which(table, devices):
        return jnp.sum(jnp.where(table[None, :] == devices[:, None], number + 1, 0), axis=1) - 1

    late = KV_HEADS - EARLY
    wide = GROUP * HEAD_DIM
    keys = key_rows.shape[1]
    slots = outgoing_slots(send, [(queries, EARLY * wide, 0), (key_rows, keys, 0)], dp_count)
    arrived_one = lax.all_to_all(slots, "dp", 0, 0, tiled=True)
    slots = outgoing_slots(send, [(queries, wide, EARLY + g) for g in range(late)], dp_count)
    arrived_two = lax.all_to_all(slots, "dp", 0, 0, tiled=True)

    width = value_weight.shape[1] // 2
    half = lax.dynamic_slice_in_dim(value_weight, core * width, width, axis=1)
    x, y = fsdp // side, fsdp % side
    line = gather_ring(half, x, side, along_x, False)
    own = gather_ring(line, y, side, along_y, True)
    own = jnp.transpose(own, (1, 0, 2, 3)).reshape(depth, width)
    (other,) = swap([own])

    onward = (((plane_at + hop_steps) % planes * 2)[:, None] + pair).reshape(-1)
    origin = (plane_at + planes - hop_steps) % planes * 2
    origin = jnp.concatenate([origin + core, origin + 1 - core])
    block = jnp.maximum(which(send, onward), 0)
    place = which(take, origin)
    doc_column = doc_ids.reshape(rows, 1)
    leaving = value_blocks(core_of, block, normed, own, other)
    landed = along_z(leaving)
    landed += swap(landed)
    packed_v = pack(core_of, place, landed, rows)

    column = 2 * jnp.arange(planes, dtype=jnp.int32)
    tile = depth // dp_count
    picked = pick_columns(column + 1 - core, normed, tile)
    (got,) = swap([picked])
    turned = turn_columns(column + core, normed, got, tile)
    (partner,) = swap([send_to])
    sends = jnp.concatenate([send_to, partner], axis=0)

    key_at = EARLY * GROUP
    done = attention(
        take, arrived_one, arrived_one, packed_v, out_grad, (doc_ids, doc_column),
        0, EARLY, key_at, (),
    )
    query_grad, key_grad, value_grad, returning = attention(
        take, arrived_two, arrived_one, packed_v, out_grad, (doc_ids, doc_column),
        EARLY, late, key_at, done,
    )
    landed = lax.all_to_all(returning, "dp", 0, 0, tiled=True)
    (swapped,) = swap([landed])
    input_grad = input_gradient(core_of, value_grad, own, other)

    chip = weight_part(sends, turned, landed, swapped, fsdp_count, planes)
    chips = lax.all_to_all(chip, "fsdp", 0, 0, tiled=True)
    plane = jnp.sum(chips.astype(jnp.float32), axis=0).astype(jnp.bfloat16)
    groups = [list(range(c, dp_count, 2)) for c in range(2)]
    parts = lax.all_to_all(plane, "dp", 0, 0, axis_index_groups=groups, tiled=True)
    weight_grad = jnp.sum(parts.astype(jnp.float32), axis=0) * grad_scale
    return (query_grad, key_grad, input_grad, weight_grad)


def solution(mesh):
    rows = P(("dp", "fsdp"), None)
    return jax.shard_map(
        local,
        mesh=mesh,
        in_specs=(rows, rows, rows, rows, P("fsdp", None), rows, rows, rows),
        out_specs=(rows, rows, rows, rows),
        check_vma=False,
    )
```
